256 devices in a mesh: gx: 16 (over z_hi, y, core), gy: 16 (over x, z_lo).
Axes of the slice: x: 4, y: 4, z: 8 (z_hi: 2, z_lo: 4; z = z_hi * 4 + z_lo), core: 2. Of those that a mesh axis runs over, the one named last changes fastest.
Arguments:
- adjoint_rhs: float32 [32, 16, 768, 128], P('gx', 'gy'), may hold values from -6 to 6
- local_inverse: bfloat16 [32, 16, 1024, 768], P('gx', 'gy')
- local_operator: bfloat16 [32, 16, 1024, 768], P('gx', 'gy')
- spill_rows: int32 [32, 16, 4, 64], P('gx', 'gy'), may hold values from 0 to 767, as said below
- coarse_basis: bfloat16 [32, 16, 64, 768], P('gx', 'gy'), may hold values from -3 to 3
- coarse_ids: int32 [32, 16, 64], P('gx', 'gy'), may hold values from 0 to 1023
- coarse_inverse: bfloat16 [1024, 1024], P(('gx', 'gy')), may hold values from -0.00030517578 to 0.00030517578
Outputs:
- adjoint_solution: float32 [32, 16, 768, 128], P('gx', 'gy')
- residual: float32 [32, 16, 768, 128], P('gx', 'gy')
The draws below stay inside these ranges and needn't reach their ends.
Inputs may be any that keep to these rules, and one draw needn't show every extreme that they name: Each list of spill_rows holds 64 distinct rows. `coarse_ids`: A coarse function may be listed more than once for a subdomain.
All inputs are finite; a program needn't handle non-finite values.
Results may differ from the reference program's by a relative error of at most 0.0041.
Values may be sent and summed in bfloat16 or wider, within the bound.
A program may use at most 64 MiB of HBM per device.

```python
import math
import jax
import jax.numpy as jnp
from jax import lax

L = 1024
H = 64
OWN = 768
R = 128
KC = 64
NC = 1024
ITERS = 1
SUBX = 32
SUBY = 16


def near_identity(key, diagonal):
    noise_scale = 0.3 / math.sqrt(OWN)
    noise = jax.random.normal(key, (SUBX, SUBY, L, OWN), jnp.float32) * noise_scale
    return noise + diagonal * jnp.eye(L, OWN, dtype=jnp.float32)


def draw_local_inverse(key, part):
    return near_identity(jax.random.fold_in(key, 11), 0.5).astype(jnp.bfloat16)


def draw_local_operator(key, part):
    return near_identity(jax.random.fold_in(key, 23), 1.0).astype(jnp.bfloat16)


def pick_rows(one_key):
    return jax.random.permutation(one_key, OWN)[:H].astype(jnp.int32)


def draw_spill_rows(key, part):
    keys = jax.random.split(jax.random.fold_in(key, 37), SUBX * SUBY * 4)
    return jax.vmap(pick_rows)(keys).reshape(SUBX, SUBY, 4, H)


def touch_ends(values, own_key, low, top_value):
    longest = values.shape.index(max(values.shape))
    spots = []
    for shift in (0, 1):
        where = [jax.random.randint(jax.random.fold_in(own_key, axis), (), 0, length) for axis, length in enumerate(values.shape)]
        where[longest] = (where[longest] + shift) % values.shape[longest]
        spots.append(tuple(where))
    return values.at[spots[0]].set(low).at[spots[1]].set(top_value)


def levels(stream_key, dims, shards, smallest, largest):
    level = 1.0
    for axis_at, parts in shards:
        steps = jax.random.uniform(jax.random.fold_in(jax.random.fold_in(stream_key, 6), axis_at), (parts,), jnp.float32, smallest / len(shards), largest / len(shards))
        level = level * jnp.repeat(jnp.exp(steps), dims[axis_at] // parts).reshape((-1,) + (1,) * (len(dims) - 1 - axis_at))
    return level


def centred(stream_key, dims, scale, limit, cuts=(), kind=jnp.bfloat16):
    values = scale * jax.random.normal(stream_key, dims, jnp.float32)
    if cuts:
        values = values * levels(stream_key, dims, cuts, -0.22, 0.18)
    return jnp.clip(values, -limit, limit).astype(kind)


def setup_inputs(seed: int = 0) -> dict:
    key_of = jax.random.split(jax.random.key(seed), 8)
    return {
        "adjoint_rhs": centred(key_of[0], (SUBX, SUBY, OWN, R), 1.0, 6.0, ((0, 16), (1, 16)), jnp.float32),
        "local_inverse": draw_local_inverse(jax.random.fold_in(key_of[7], 71), 0),
        "local_operator": draw_local_operator(jax.random.fold_in(key_of[7], 71), 0),
        "spill_rows": draw_spill_rows(jax.random.fold_in(key_of[7], 71), 0),
        "coarse_basis": centred(key_of[4], (SUBX, SUBY, KC, OWN), 0.5, 3.0, ((0, 16), (1, 16))),
        "coarse_ids": touch_ends(jax.random.randint(key_of[5], (SUBX, SUBY, KC), 0, NC), jax.random.fold_in(key_of[5], 1), 0, NC - 1).astype(jnp.int32),
        "coarse_inverse": centred(key_of[6], (NC, NC), (KC * KC * OWN * SUBX * SUBY // 4) ** -0.5, 0.00030517578, ((0, 256),)),
    }


def from_lower(values, axis):
    zeros = jnp.zeros_like(lax.slice_in_dim(values, 0, 1, axis=axis))
    kept = lax.slice_in_dim(values, 0, values.shape[axis] - 1, axis=axis)
    return jnp.concatenate([zeros, kept], axis)


def from_upper(values, axis):
    zeros = jnp.zeros_like(lax.slice_in_dim(values, 0, 1, axis=axis))
    kept = lax.slice_in_dim(values, 1, values.shape[axis], axis=axis)
    return jnp.concatenate([kept, zeros], axis)


def add_rows(owned_rows, indices, values):
    return owned_rows.at[indices].add(values)


def spread(extended, spill_rows):
    owned_rows = extended[:, :, :OWN]
    groups = extended[:, :, OWN:].reshape(SUBX, SUBY, 4, H, R)
    from_west = from_lower(groups[:, :, 1], 0)
    from_east = from_upper(groups[:, :, 0], 0)
    from_south = from_lower(groups[:, :, 3], 1)
    from_north = from_upper(groups[:, :, 2], 1)
    received = jnp.stack([from_west, from_east, from_south, from_north], 2).reshape(SUBX * SUBY, 4 * H, R)
    indices = spill_rows.reshape(SUBX * SUBY, 4 * H)
    summed = jax.vmap(add_rows)(owned_rows.reshape(SUBX * SUBY, OWN, R), indices, received)
    return summed.reshape(SUBX, SUBY, OWN, R)


def block_product(pair):
    return jnp.dot(pair[0], pair[1], preferred_element_type=jnp.float32)


def apply_blocks(matrices, vectors):
    flat = lax.map(block_product, (matrices.reshape(SUBX * SUBY, L, OWN), vectors.astype(jnp.bfloat16).reshape(SUBX * SUBY, OWN, R)))
    return flat.reshape(SUBX, SUBY, L, R)


def reference(adjoint_rhs, local_inverse, local_operator, spill_rows, coarse_basis, coarse_ids, coarse_inverse):
    highest = lax.Precision.HIGHEST
    basis_rows = coarse_basis.astype(jnp.float32)
    residual = adjoint_rhs
    solution = jnp.zeros_like(adjoint_rhs)
    for iteration in range(ITERS):
        local_sol = apply_blocks(local_inverse, residual)
        terms = jnp.einsum('xykn,xynr->xykr', basis_rows, residual, precision=highest)
        coarse_rhs = jnp.zeros((NC, R), jnp.float32).at[coarse_ids.reshape(-1)].add(terms.reshape(-1, R))
        coarse_sol = jnp.dot(coarse_inverse.T, coarse_rhs.astype(jnp.bfloat16), preferred_element_type=jnp.float32)
        picked = coarse_sol[coarse_ids]
        coarse_part = jnp.einsum('xykn,xykr->xynr', basis_rows, picked, precision=highest)
        correction = spread(local_sol, spill_rows) + coarse_part
        solution = solution + correction
        image = apply_blocks(local_operator, correction)
        residual = residual - spread(image, spill_rows)
    return solution, residual
```

```python
import functools

import jax
import jax.numpy as jnp
from jax import lax
from jax.experimental import pallas as pl
from jax.experimental.pallas import tpu as pltpu
from jax.sharding import PartitionSpec as P

F32 = jnp.float32
BF16 = jnp.bfloat16
MESH = pl.DeviceIdType.MESH
OWN = 768
H = 64
R = 128
KC = 64
NC = 1024
XS, YS, ZS = 4, 4, 8


def dot(a, b):
    return jnp.dot(a, b, preferred_element_type=F32)


def dot_first(a, b):
    return lax.dot_general(a, b, (((0,), (0,)), ((), ())), preferred_element_type=F32)


def split(value):
    high = value.astype(BF16)
    return high, (value - high.astype(F32)).astype(BF16)


def ring_distance(step, size):
    return min(step, size - step)


PLANE = sorted(
    [(dx, dy, dc) for dx in range(XS) for dy in range(YS) for dc in range(2) if (dx, dy, dc) != (0, 0, 0)],
    key=lambda o: -(ring_distance(o[0], XS) + ring_distance(o[1], YS)),
)
RING = sorted(range(1, ZS), key=lambda dz: -ring_distance(dz, ZS))


def kernel(
    rhs_hbm, inv_hbm, op_hbm, spill_hbm, basis_hbm, ids_hbm, cinv_hbm,
    sol_hbm, res_hbm,
    rhs, inv, op, spill, basis, ids, cz, cf,
    sbuf, rbuf, zs, zr, low,
    mbuf, marg, mbuf2, marg2, spread_mat, basis_t, wsel,
    corr, out_sol, out_res,
    load_sem, rs_send, rs_recv, z_send, z_recv, ag_send, ag_recv,
    cz_send, cz_recv, c2_send, c2_recv, c3_send, c3_recv, c4_send, c4_recv,
    m_send, m_recv, n_send, n_recv, store_sem,
):
    gx, gy = lax.axis_index("gx"), lax.axis_index("gy")
    core = lax.rem(gx, 2)
    y = lax.rem(lax.div(gx, 2), YS)
    x = lax.div(gy, 4)
    z = lax.div(gx, 8) * 4 + lax.rem(gy, 4)

    def device(xx, yy, zz, cc):
        return (lax.div(zz, 4) * 8 + yy * 2 + cc, xx * 4 + lax.rem(zz, 4))

    def plane_peer(offset):
        dx, dy, dc = offset
        xx, yy, cc = lax.rem(x + dx, XS), lax.rem(y + dy, YS), lax.rem(core + dc, 2)
        return (yy * 2 + cc) * 4 + xx, device(xx, yy, z, cc)

    def ring_peer(dz):
        return device(x, y, lax.rem(z + dz, ZS), core)

    def x_peer(dx):
        return device(lax.rem(x + dx, XS), y, z, core)

    def y_peer(dy):
        return device(x, lax.rem(y + dy, YS), z, core)

    partner = (gx + 1 - 2 * core, gy)
    east = (lax.rem(gx + 1, 16), gy)
    west = (lax.rem(gx + 15, 16), gy)
    north = (gx, lax.rem(gy + 1, 16))
    south = (gx, lax.rem(gy + 15, 16))
    mine = (y * 2 + core) * 4 + x

    def load(source, target, index):
        copy = pltpu.make_async_copy(source, target, load_sem.at[index])
        copy.start()
        return copy

    load_ids = load(ids_hbm, ids, 0)
    load_rhs = load(rhs_hbm, rhs, 1)
    load_basis = load(basis_hbm, basis, 2)
    load_cinv = load(cinv_hbm, cz.at[z], 3)
    load_inv = load(inv_hbm, inv, 4)
    load_spill = load(spill_hbm, spill, 5)
    load_op = load(op_hbm, op, 6)

    barrier = pltpu.get_barrier_semaphore()
    greeted = [plane_peer(o)[1] for o in PLANE] + [ring_peer(d) for d in RING] + [east, west, north, south]
    for peer in greeted:
        pl.semaphore_signal(barrier, inc=1, device_id=peer, device_id_type=MESH)

    def send(source, target, send_sem, recv_sem, peer):
        pltpu.make_async_remote_copy(
            src_ref=source, dst_ref=target, send_sem=send_sem, recv_sem=recv_sem,
            device_id=peer, device_id_type=MESH,
        ).start()

    def drain(ref, sem):
        pltpu.make_async_copy(ref, ref, sem).wait()

    load_ids.wait()
    load_rhs.wait()
    load_basis.wait()
    numbers = jnp.concatenate([ids[0], ids[1]], axis=1)
    places = ((numbers & 496) << 1) | ((numbers >> 9) << 4) | (numbers & 15)
    rows = lax.broadcasted_iota(jnp.int32, (NC, 2 * KC), 0)
    scatter = jnp.where(rows == places, 1.0, 0.0).astype(BF16)
    terms = []
    for s in range(2):
        high, rest = split(rhs[s, 0])
        terms.append(dot(basis[s, 0], high) + dot(basis[s, 0], rest))
    high, rest = split(jnp.concatenate(terms, axis=0))
    local_sums = dot(scatter, high) + dot(scatter, rest)
    sbuf[...] = local_sums.astype(BF16).reshape(32, 32, R)

    pl.semaphore_wait(barrier, len(greeted))
    for slot, offset in enumerate(PLANE):
        block, peer = plane_peer(offset)
        send(sbuf.at[block], rbuf.at[slot], rs_send, rs_recv, peer)
    load_cinv.wait()
    for dz in RING:
        send(cz.at[z], cz.at[z], cz_send, cz_recv, ring_peer(dz))

    load_inv.wait()
    heads = [rhs[s, 0].astype(BF16) for s in range(2)]
    for s in range(2):
        edge = dot(inv[s, 0, OWN:, :], heads[s]).astype(BF16).reshape(4, H, R)
        mbuf[s] = edge
        marg[1 - s, s] = edge[1 - s]
    send(mbuf.at[1, 1], marg.at[0, 0], m_send, m_recv, east)
    send(mbuf.at[0, 0], marg.at[1, 1], m_send, m_recv, west)
    send(mbuf.at[:, 3], marg.at[:, 2], m_send, m_recv, north)
    send(mbuf.at[:, 2], marg.at[:, 3], m_send, m_recv, south)
    for s in range(2):
        corr[s] = dot(inv[s, 0, :OWN, :], heads[s])
    load_spill.wait()
    for s in range(2):
        listed = spill[s, 0]
        listed = jnp.concatenate([listed[d : d + 1] for d in range(4)], axis=1)
        owned = lax.broadcasted_iota(jnp.int32, (OWN, 4 * H), 0)
        spread_mat[s] = jnp.where(owned == listed, 1.0, 0.0).astype(BF16)
        basis_t[s] = basis[s, 0].T
    pick = jnp.where(rows == numbers, 1.0, 0.0).astype(BF16)

    drain(cz.at[0:7], cz_recv)
    cf[y, core, x] = jnp.concatenate([cz[i].astype(F32) for i in range(ZS)], axis=0).astype(BF16)
    for d in (2, 1, 3):
        send(cf.at[y, core, x, 0:16], cf.at[y, core, x, 0:16], c2_send.at[0], c2_recv.at[0], x_peer(d))
        send(cf.at[y, core, x, 16:32], cf.at[y, core, x, 16:32], c2_send.at[1], c2_recv.at[1], y_peer(d))

    drain(rbuf, rs_recv)
    total = sbuf[mine].astype(F32)
    for slot in range(31):
        total = total + rbuf[slot].astype(F32)
    zs[...] = total.astype(BF16)
    for slot, dz in enumerate(RING):
        send(zs, zr.at[slot], z_send, z_recv, ring_peer(dz))

    drain(cf.at[0, 0, 0:3, 0:16], c2_recv.at[0])
    drain(cf.at[0, 0, 0:3, 0:16], c2_recv.at[1])
    for d in (2, 1, 3):
        send(cf.at[y, core, :, 0:16], cf.at[y, core, :, 0:16], c3_send.at[0], c3_recv.at[0], y_peer(d))
        send(cf.at[:, core, x, 16:32], cf.at[:, core, x, 16:32], c3_send.at[1], c3_recv.at[1], x_peer(d))

    def kept(values):
        return [
            (jnp.where(gx > 0, values[0, 0], 0), values[0, 1], jnp.where(gy > 0, values[0, 2], 0),
             jnp.where(gy < 15, values[0, 3], 0)),
            (values[1, 0], jnp.where(gx < 15, values[1, 1], 0), jnp.where(gy > 0, values[1, 2], 0),
             jnp.where(gy < 15, values[1, 3], 0)),
        ]

    drain(mbuf.at[:, 0:3], m_recv)
    received = kept(marg)
    for s in range(2):
        corr[s] = corr[s] + dot(spread_mat[s], jnp.concatenate(received[s], axis=0))

    drain(zr, z_recv)
    total = total.astype(BF16).astype(F32)
    for slot in range(7):
        total = total + zr[slot].astype(F32)
    low[mine] = total.astype(BF16)
    for offset in PLANE:
        send(low.at[mine], low.at[mine], ag_send, ag_recv, plane_peer(offset)[1])

    drain(cf.at[0:3, 0, :, 0:16], c3_recv.at[0])
    drain(cf.at[0:3, 0, :, 0:16], c3_recv.at[1])
    send(cf.at[:, core], cf.at[:, core], c4_send, c4_recv, partner)
    drain(cf.at[:, 0], c4_recv)
    wsel[...] = dot(cf[...].reshape(NC, NC), pick).astype(BF16)

    load_op.wait()
    drain(low.at[0:31], ag_recv)
    picked = dot_first(wsel[...], low[...].reshape(NC, R))
    for s in range(2):
        high, rest = split(picked[s * KC : (s + 1) * KC])
        value = corr[s] + (dot(basis_t[s], high) + dot(basis_t[s], rest))
        out_sol[s, 0] = value
        heads[s] = value.astype(BF16)
        edge = dot(op[s, 0, OWN:, :], heads[s]).astype(BF16).reshape(4, H, R)
        mbuf2[s] = edge
        marg2[1 - s, s] = edge[1 - s]
    send(mbuf2.at[1, 1], marg2.at[0, 0], n_send, n_recv, east)
    send(mbuf2.at[0, 0], marg2.at[1, 1], n_send, n_recv, west)
    send(mbuf2.at[:, 3], marg2.at[:, 2], n_send, n_recv, north)
    send(mbuf2.at[:, 2], marg2.at[:, 3], n_send, n_recv, south)
    store_sol = pltpu.make_async_copy(out_sol, sol_hbm, store_sem.at[0])
    store_sol.start()
    for s in range(2):
        corr[s] = rhs[s, 0] - dot(op[s, 0, :OWN, :], heads[s])
    drain(mbuf2.at[:, 0:3], n_recv)
    received = kept(marg2)
    for s in range(2):
        out_res[s, 0] = corr[s] - dot(spread_mat[s], jnp.concatenate(received[s], axis=0))
    store_res = pltpu.make_async_copy(out_res, res_hbm, store_sem.at[1])
    store_res.start()

    drain(rbuf, rs_send)
    drain(zr, z_send)
    drain(low.at[0:31], ag_send)
    drain(cz.at[0:7], cz_send)
    for i in range(2):
        drain(cf.at[0, 0, 0:3, 0:16], c2_send.at[i])
        drain(cf.at[0:3, 0, :, 0:16], c3_send.at[i])
    drain(cf.at[:, 0], c4_send)
    drain(mbuf.at[:, 0:3], m_send)
    drain(mbuf2.at[:, 0:3], n_send)
    store_sol.wait()
    store_res.wait()


def body(adjoint_rhs, local_inverse, local_operator, spill_rows, coarse_basis, coarse_ids, coarse_inverse):
    anywhere = pl.BlockSpec(memory_space=pl.ANY)
    dma = pltpu.SemaphoreType.DMA
    out = jax.ShapeDtypeStruct(adjoint_rhs.shape, F32)
    return pl.pallas_call(
        kernel,
        out_shape=(out, out),
        in_specs=[anywhere] * 7,
        out_specs=(anywhere, anywhere),
        scratch_shapes=[
            pltpu.VMEM(adjoint_rhs.shape, F32),
            pltpu.VMEM(local_inverse.shape, BF16),
            pltpu.VMEM(local_operator.shape, BF16),
            pltpu.VMEM(spill_rows.shape, jnp.int32),
            pltpu.VMEM(coarse_basis.shape, BF16),
            pltpu.VMEM(coarse_ids.shape, jnp.int32),
            pltpu.VMEM((ZS, 4, NC), BF16),
            pltpu.VMEM((4, 2, 4, 32, NC), BF16),
            pltpu.VMEM((32, 32, R), BF16),
            pltpu.VMEM((31, 32, R), BF16),
            pltpu.VMEM((32, R), BF16),
            pltpu.VMEM((7, 32, R), BF16),
            pltpu.VMEM((32, 32, R), BF16),
            pltpu.VMEM((2, 4, H, R), BF16),
            pltpu.VMEM((2, 4, H, R), BF16),
            pltpu.VMEM((2, 4, H, R), BF16),
            pltpu.VMEM((2, 4, H, R), BF16),
            pltpu.VMEM((2, OWN, 4 * H), BF16),
            pltpu.VMEM((2, OWN, KC), BF16),
            pltpu.VMEM((NC, 2 * KC), BF16),
            pltpu.VMEM((2, OWN, R), F32),
            pltpu.VMEM(adjoint_rhs.shape, F32),
            pltpu.VMEM(adjoint_rhs.shape, F32),
            dma((7,)),
            dma(()), dma(()), dma(()), dma(()), dma(()), dma(()),
            dma(()), dma(()), dma((2,)), dma((2,)), dma((2,)), dma((2,)), dma(()), dma(()),
            dma(()), dma(()), dma(()), dma(()), dma((2,)),
        ],
        compiler_params=pltpu.CompilerParams(
            collective_id=0, has_side_effects=True, vmem_limit_bytes=48 * 1024 * 1024
        ),
    )(adjoint_rhs, local_inverse, local_operator, spill_rows, coarse_basis, coarse_ids, coarse_inverse)


def solution(mesh):
    in_specs = (
        P("gx", "gy", None, None),
        P("gx", "gy", None, None),
        P("gx", "gy", None, None),
        P("gx", "gy", None, None),
        P("gx", "gy", None, None),
        P("gx", "gy", None),
        P(("gx", "gy"), None),
    )
    out_specs = (P("gx", "gy", None, None), P("gx", "gy", None, None))
    return jax.shard_map(body, mesh=mesh, in_specs=in_specs, out_specs=out_specs, check_vma=False)
```

```python
import functools

import jax
import jax.numpy as jnp
from jax import lax
from jax.experimental import pallas as pl
from jax.experimental.pallas import tpu as pltpu
from jax.sharding import PartitionSpec as P

F32 = jnp.float32
BF16 = jnp.bfloat16
MESH = pl.DeviceIdType.MESH
OWN = 768
H = 64
R = 128
KC = 64
NC = 1024
XS, YS, ZS = 4, 4, 8


def dot(a, b):
    return jnp.dot(a, b, preferred_element_type=F32)


def dot_first(a, b):
    return lax.dot_general(a, b, (((0,), (0,)), ((), ())), preferred_element_type=F32)


def split(value):
    high = value.astype(BF16)
    return high, (value - high.astype(F32)).astype(BF16)


def ring_distance(step, size):
    return min(step, size - step)


PLANE = sorted(
    [(dx, dy, dc) for dx in range(XS) for dy in range(YS) for dc in range(2) if (dx, dy, dc) != (0, 0, 0)],
    key=lambda o: -(ring_distance(o[0], XS) + ring_distance(o[1], YS)),
)
RING = sorted(range(1, ZS), key=lambda dz: -ring_distance(dz, ZS))


def kernel(
    rhs_hbm, inv_hbm, op_hbm, spill_hbm, basis_hbm, ids_hbm, cinv_hbm,
    out_sol, out_res,
    rhs, inv, op, spill, basis, ids, cz, cf,
    sbuf, rbuf, zs, zr, low,
    mbuf, marg, mbuf2, marg2, nids, spread_mat, basis_t, qmat, pick, wsel,
    corr, prior,
    load_sem, rs_send, rs_recv, z_send, z_recv, ag_send, ag_recv,
    cz_send, cz_recv, c2_send, c2_recv, c3_send, c3_recv, c4_send, c4_recv,
    m_send, m_recv, n_send, n_recv, i_send, i_recv,
):
    gx, gy = lax.axis_index("gx"), lax.axis_index("gy")
    core = lax.rem(gx, 2)
    y = lax.rem(lax.div(gx, 2), YS)
    x = lax.div(gy, 4)
    z = lax.div(gx, 8) * 4 + lax.rem(gy, 4)

    def device(xx, yy, zz, cc):
        return (lax.div(zz, 4) * 8 + yy * 2 + cc, xx * 4 + lax.rem(zz, 4))

    def plane_peer(offset):
        dx, dy, dc = offset
        xx, yy, cc = lax.rem(x + dx, XS), lax.rem(y + dy, YS), lax.rem(core + dc, 2)
        return (yy * 2 + cc) * 4 + xx, device(xx, yy, z, cc)

    def ring_peer(dz):
        return device(x, y, lax.rem(z + dz, ZS), core)

    def x_peer(dx):
        return device(lax.rem(x + dx, XS), y, z, core)

    def y_peer(dy):
        return device(x, lax.rem(y + dy, YS), z, core)

    partner = (gx + 1 - 2 * core, gy)
    east = (lax.rem(gx + 1, 16), gy)
    west = (lax.rem(gx + 15, 16), gy)
    north = (gx, lax.rem(gy + 1, 16))
    south = (gx, lax.rem(gy + 15, 16))
    mine = (y * 2 + core) * 4 + x

    def load(source, target, index):
        copy = pltpu.make_async_copy(source, target, load_sem.at[index])
        copy.start()
        return copy

    load_ids = load(ids_hbm, ids, 0)
    load_rhs = load(rhs_hbm, rhs, 1)
    load_basis = load(basis_hbm, basis, 2)
    load_cinv = load(cinv_hbm, cz.at[z], 3)
    load_inv = load(inv_hbm, inv, 4)
    load_spill = load(spill_hbm, spill, 5)
    load_op = load(op_hbm, op, 6)

    barrier = pltpu.get_barrier_semaphore()
    greeted = [plane_peer(o)[1] for o in PLANE] + [ring_peer(d) for d in RING] + [east, west, north, south]
    for peer in greeted:
        pl.semaphore_signal(barrier, inc=1, device_id=peer, device_id_type=MESH)

    def send(source, target, send_sem, recv_sem, peer):
        pltpu.make_async_remote_copy(
            src_ref=source, dst_ref=target, send_sem=send_sem, recv_sem=recv_sem,
            device_id=peer, device_id_type=MESH,
        ).start()

    def drain(ref, sem):
        pltpu.make_async_copy(ref, ref, sem).wait()

    def exchange(source, target, send_sem, recv_sem):
        send(source.at[1, 1], target.at[0, 0], send_sem, recv_sem, east)
        send(source.at[0, 0], target.at[1, 1], send_sem, recv_sem, west)
        send(source.at[:, 3], target.at[:, 2], send_sem, recv_sem, north)
        send(source.at[:, 2], target.at[:, 3], send_sem, recv_sem, south)

    def kept(values):
        return [
            (jnp.where(gx > 0, values[0, 0], 0), values[0, 1], jnp.where(gy > 0, values[0, 2], 0),
             jnp.where(gy < 15, values[0, 3], 0)),
            (values[1, 0], jnp.where(gx < 15, values[1, 1], 0), jnp.where(gy > 0, values[1, 2], 0),
             jnp.where(gy < 15, values[1, 3], 0)),
        ]

    load_ids.wait()
    load_rhs.wait()
    load_basis.wait()
    numbers = jnp.concatenate([ids[0], ids[1]], axis=1)
    places = ((numbers & 496) << 1) | ((numbers >> 9) << 4) | (numbers & 15)
    rows = lax.broadcasted_iota(jnp.int32, (NC, 2 * KC), 0)
    scatter = jnp.where(rows == places, 1.0, 0.0).astype(BF16)
    terms = []
    for s in range(2):
        high, rest = split(rhs[s, 0])
        terms.append(dot(basis[s, 0], high) + dot(basis[s, 0], rest))
    high, rest = split(jnp.concatenate(terms, axis=0))
    local_sums = dot(scatter, high) + dot(scatter, rest)
    sbuf[...] = local_sums.astype(BF16).reshape(32, 32, R)

    pl.semaphore_wait(barrier, len(greeted))
    for slot, offset in enumerate(PLANE):
        block, peer = plane_peer(offset)
        send(sbuf.at[block], rbuf.at[slot], rs_send, rs_recv, peer)
    load_cinv.wait()
    for dz in RING:
        send(cz.at[z], cz.at[z], cz_send, cz_recv, ring_peer(dz))
    send(ids.at[1], nids.at[0], i_send, i_recv, east)
    send(ids.at[0], nids.at[1], i_send, i_recv, west)
    send(ids, nids.at[2:4], i_send, i_recv, north)
    send(ids, nids.at[4:6], i_send, i_recv, south)

    load_inv.wait()
    heads = [rhs[s, 0].astype(BF16) for s in range(2)]
    for s in range(2):
        edge = dot(inv[s, 0, OWN:, :], heads[s]).astype(BF16).reshape(4, H, R)
        mbuf[s] = edge
        marg[1 - s, s] = edge[1 - s]
    exchange(mbuf, marg, m_send, m_recv)
    for s in range(2):
        corr[s] = dot(inv[s, 0, :OWN, :], heads[s])
    load_spill.wait()
    for s in range(2):
        listed = spill[s, 0]
        listed = jnp.concatenate([listed[d : d + 1] for d in range(4)], axis=1)
        owned = lax.broadcasted_iota(jnp.int32, (OWN, 4 * H), 0)
        spread_mat[s] = jnp.where(owned == listed, 1.0, 0.0).astype(BF16)
        basis_t[s] = jnp.concatenate([basis[s, 0], basis[s, 0]], axis=0).T
    load_op.wait()
    left = lax.broadcasted_iota(jnp.int32, (H, R), 1) < KC
    for s in range(2):
        edge = dot(op[s, 0, OWN:, :], basis_t[s]).reshape(4, H, R)
        for d in range(4):
            half = jnp.where(left if d in (1, 3) else ~left, edge[d], 0.0).astype(BF16)
            mbuf2[s, d, 1] = half
            if d == 1 - s:
                marg2[1 - s, s, 1] = half
        qmat[s, :, 0:R] = dot(op[s, 0, :OWN, :], basis_t[s]).astype(BF16)

    drain(cz.at[0:7], cz_recv)
    cf[y, core, x] = jnp.concatenate([cz[i].astype(F32) for i in range(ZS)], axis=0).astype(BF16)
    first, second = slice(0, 16), slice(16, 32)
    for d in (2, 1, 3):
        send(cf.at[y, core, x, first], cf.at[y, core, x, first], c2_send.at[0], c2_recv.at[0], x_peer(d))
        send(cf.at[y, core, x, second], cf.at[y, core, x, second], c2_send.at[1], c2_recv.at[1], y_peer(d))
    for d in (2, 1, 3):
        send(cf.at[y, core, x, first], cf.at[y, core, x, first], c3_send.at[0], c3_recv.at[0], y_peer(d))
        send(cf.at[y, core, x, second], cf.at[y, core, x, second], c3_send.at[1], c3_recv.at[1], x_peer(d))

    drain(rbuf, rs_recv)
    total = sbuf[mine].astype(F32)
    for slot in range(31):
        total = total + rbuf[slot].astype(F32)
    zs[...] = total.astype(BF16)
    for slot, dz in enumerate(RING):
        send(zs, zr.at[slot], z_send, z_recv, ring_peer(dz))

    drain(mbuf.at[:, 0:3], m_recv)
    received = kept(marg)
    for s in range(2):
        corr[s] = corr[s] + dot(spread_mat[s], jnp.concatenate(received[s], axis=0))
        heads[s] = corr[s].astype(BF16)
        edge = dot(op[s, 0, OWN:, :], heads[s]).astype(BF16).reshape(4, H, R)
        for d in range(4):
            mbuf2[s, d, 0] = edge[d]
        marg2[1 - s, s, 0] = edge[1 - s]
    exchange(mbuf2, marg2, n_send, n_recv)

    drain(cf.at[0, 0, 0:3, first], c2_recv.at[0])
    drain(cf.at[0, 0, 0:3, first], c2_recv.at[1])
    for other in (1, 2, 3):
        xx, yy = lax.rem(x + other, XS), lax.rem(y + other, YS)
        for d in (2, 1, 3):
            send(cf.at[y, core, xx, first], cf.at[y, core, xx, first], c3_send.at[0], c3_recv.at[0], y_peer(d))
            send(cf.at[yy, core, x, second], cf.at[yy, core, x, second], c3_send.at[1], c3_recv.at[1], x_peer(d))
    for s in range(2):
        prior[s] = rhs[s, 0] - dot(op[s, 0, :OWN, :], heads[s])

    drain(zr, z_recv)
    total = total.astype(BF16).astype(F32)
    for slot in range(7):
        total = total + zr[slot].astype(F32)
    low[mine] = total.astype(BF16)
    for offset in PLANE:
        send(low.at[mine], low.at[mine], ag_send, ag_recv, plane_peer(offset)[1])

    drain(nids, i_recv)
    numbers = jnp.concatenate([ids[0], ids[1]] + [nids[i] for i in range(6)], axis=1)
    rows = lax.broadcasted_iota(jnp.int32, (NC, 8 * KC), 0)
    pick[...] = jnp.where(rows == numbers, 1.0, 0.0).astype(BF16)
    drain(mbuf2.at[:, 0:3], n_recv)
    for s in range(2):
        arrived = [
            jnp.where(gx > 0, marg2[0, 0], 0) if s == 0 else marg2[1, 0],
            marg2[0, 1] if s == 0 else jnp.where(gx < 15, marg2[1, 1], 0),
            jnp.where(gy > 0, marg2[s, 2], 0),
            jnp.where(gy < 15, marg2[s, 3], 0),
        ]
        prior[s] = prior[s] - dot(spread_mat[s], jnp.concatenate([a[0] for a in arrived], axis=0))
        for half in range(2):
            pair = jnp.concatenate([arrived[2 * half][1], arrived[2 * half + 1][1]], axis=0)
            lanes = slice(R * (half + 1), R * (half + 2))
            qmat[s, :, lanes] = dot(spread_mat[s, :, R * half : R * (half + 1)], pair).astype(BF16)

    drain(cf.at[0:3, 0, :, first], c3_recv.at[0])
    drain(cf.at[0:3, 0, :, first], c3_recv.at[1])
    send(cf.at[:, core], cf.at[:, core], c4_send, c4_recv, partner)
    drain(cf.at[:, 0], c4_recv)
    wsel[...] = dot(cf[...].reshape(NC, NC), pick[...]).astype(BF16).T

    drain(low.at[0:31], ag_recv)
    picked = dot(wsel[...], low[...].reshape(NC, R))
    parts = [picked[i * KC : (i + 1) * KC].astype(BF16) for i in range(8)]
    beside = ((2, 1, 4, 6), (0, 3, 5, 7))
    for s in range(2):
        high, rest = split(picked[s * KC : (s + 1) * KC])
        both = jnp.concatenate([high, rest], axis=0)
        out_sol[s, 0] = corr[s] + dot(basis_t[s], both)
        stack = jnp.concatenate([both] + [parts[i] for i in beside[s]], axis=0)
        out_res[s, 0] = prior[s] - dot(qmat[s], stack)

    drain(rbuf, rs_send)
    drain(zr, z_send)
    drain(low.at[0:31], ag_send)
    drain(cz.at[0:7], cz_send)
    drain(nids, i_send)
    for i in range(2):
        drain(cf.at[0, 0, 0:3, first], c2_send.at[i])
        drain(cf.at[0:3, 0, :, first], c3_send.at[i])
    drain(cf.at[:, 0], c4_send)
    drain(mbuf.at[:, 0:3], m_send)
    drain(mbuf2.at[:, 0:3], n_send)


def deliver(sol_ref, res_ref, sol_out, res_out, sem):
    copies = [
        pltpu.make_async_copy(sol_ref, sol_out, sem.at[0]),
        pltpu.make_async_copy(res_ref, res_out, sem.at[1]),
    ]
    for copy in copies:
        copy.start()
    for copy in copies:
        copy.wait()


def body(adjoint_rhs, local_inverse, local_operator, spill_rows, coarse_basis, coarse_ids, coarse_inverse):
    anywhere = pl.BlockSpec(memory_space=pl.ANY)
    hbm = pl.BlockSpec(memory_space=pltpu.HBM)
    vmem = pl.BlockSpec(memory_space=pltpu.VMEM)
    dma = pltpu.SemaphoreType.DMA
    out = jax.ShapeDtypeStruct(adjoint_rhs.shape, F32)
    operands = (
        adjoint_rhs, local_inverse, local_operator, spill_rows, coarse_basis, coarse_ids, coarse_inverse
    )
    results = pl.pallas_call(
        kernel,
        out_shape=(out, out),
        in_specs=[hbm] * 7,
        out_specs=(vmem, vmem),
        scratch_shapes=[
            pltpu.VMEM(adjoint_rhs.shape, F32),
            pltpu.VMEM(local_inverse.shape, BF16),
            pltpu.VMEM(local_operator.shape, BF16),
            pltpu.VMEM(spill_rows.shape, jnp.int32),
            pltpu.VMEM(coarse_basis.shape, BF16),
            pltpu.VMEM(coarse_ids.shape, jnp.int32),
            pltpu.VMEM((ZS, 4, NC), BF16),
            pltpu.VMEM((4, 2, 4, 32, NC), BF16),
            pltpu.VMEM((32, 32, R), BF16),
            pltpu.VMEM((31, 32, R), BF16),
            pltpu.VMEM((32, R), BF16),
            pltpu.VMEM((7, 32, R), BF16),
            pltpu.VMEM((32, 32, R), BF16),
            pltpu.VMEM((2, 4, H, R), BF16),
            pltpu.VMEM((2, 4, H, R), BF16),
            pltpu.VMEM((2, 4, 2, H, R), BF16),
            pltpu.VMEM((2, 4, 2, H, R), BF16),
            pltpu.VMEM((6, 1, KC), jnp.int32),
            pltpu.VMEM((2, OWN, 4 * H), BF16),
            pltpu.VMEM((2, OWN, R), BF16),
            pltpu.VMEM((2, OWN, 3 * R), BF16),
            pltpu.VMEM((NC, 8 * KC), BF16),
            pltpu.VMEM((8 * KC, NC), BF16),
            pltpu.VMEM((2, OWN, R), F32),
            pltpu.VMEM((2, OWN, R), F32),
            dma((7,)),
            dma(()), dma(()), dma(()), dma(()), dma(()), dma(()),
            dma(()), dma(()), dma((2,)), dma((2,)), dma((2,)), dma((2,)), dma(()), dma(()),
            dma(()), dma(()), dma(()), dma(()), dma(()), dma(()),
        ],
        compiler_params=pltpu.CompilerParams(
            collective_id=0, has_side_effects=True, vmem_limit_bytes=48 * 1024 * 1024
        ),
    )(*[pltpu.with_memory_space_constraint(a, pltpu.HBM) for a in operands])
    return pl.pallas_call(
        deliver,
        out_shape=(out, out),
        in_specs=[anywhere] * 2,
        out_specs=(hbm, hbm),
        scratch_shapes=[dma((2,))],
        compiler_params=pltpu.CompilerParams(vmem_limit_bytes=16 * 1024 * 1024),
    )(*results)


def solution(mesh):
    in_specs = (
        P("gx", "gy", None, None),
        P("gx", "gy", None, None),
        P("gx", "gy", None, None),
        P("gx", "gy", None, None),
        P("gx", "gy", None, None),
        P("gx", "gy", None),
        P(("gx", "gy"), None),
    )
    out_specs = (P("gx", "gy", None, None), P("gx", "gy", None, None))
    return jax.shard_map(body, mesh=mesh, in_specs=in_specs, out_specs=out_specs, check_vma=False)
```

```python
import functools

import jax
import jax.numpy as jnp
from jax import lax
from jax.experimental import pallas as pl
from jax.experimental.pallas import tpu as pltpu
from jax.sharding import PartitionSpec as P

F32 = jnp.float32
BF16 = jnp.bfloat16
MESH = pl.DeviceIdType.MESH
OWN = 768
H = 64
R = 128
KC = 64
NC = 1024
XS, YS, ZS = 4, 4, 8


def dot(a, b):
    return jnp.dot(a, b, preferred_element_type=F32)


def dot_first(a, b):
    return lax.dot_general(a, b, (((0,), (0,)), ((), ())), preferred_element_type=F32)


def split(value):
    high = value.astype(BF16)
    return high, (value - high.astype(F32)).astype(BF16)


def ring_distance(step, size):
    return min(step, size - step)


PLANE = sorted(
    [(dx, dy, dc) for dx in range(XS) for dy in range(YS) for dc in range(2) if (dx, dy, dc) != (0, 0, 0)],
    key=lambda o: -(ring_distance(o[0], XS) + ring_distance(o[1], YS)),
)
RING = sorted(range(1, ZS), key=lambda dz: -ring_distance(dz, ZS))


def kernel(
    rhs_hbm, inv_hbm, op_hbm, spill_hbm, basis_hbm, ids_hbm, cinv_hbm,
    corr, prior, basis_t, qmat, picked,
    rhs, inv, op, spill, basis, ids, cz, cf,
    sbuf, rbuf, zs, zr, low,
    mbuf, marg, mbuf2, marg2, nids, spread_mat, pick, wsel, lists, trade,
    load_sem, rs_send, rs_recv, z_send, z_recv, ag_send, ag_recv,
    cz_send, cz_recv, c2_send, c2_recv, c3_send, c3_recv, c4_send, c4_recv,
    m_send, m_recv, n_send, n_recv, i_send, i_recv, l_send, l_recv,
):
    gx, gy = lax.axis_index("gx"), lax.axis_index("gy")

    core = lax.rem(gx, 2)
    y = lax.rem(lax.div(gx, 2), YS)
    x = lax.div(gy, 4)
    z = lax.div(gx, 8) * 4 + lax.rem(gy, 4)

    def device(xx, yy, zz, cc):
        return (lax.div(zz, 4) * 8 + yy * 2 + cc, xx * 4 + lax.rem(zz, 4))

    def plane_peer(offset):
        dx, dy, dc = offset
        xx, yy, cc = lax.rem(x + dx, XS), lax.rem(y + dy, YS), lax.rem(core + dc, 2)
        return (yy * 2 + cc) * 4 + xx, device(xx, yy, z, cc)

    def ring_peer(dz):
        return device(x, y, lax.rem(z + dz, ZS), core)

    def x_peer(dx):
        return device(lax.rem(x + dx, XS), y, z, core)

    def y_peer(dy):
        return device(x, lax.rem(y + dy, YS), z, core)

    partner = (gx + 1 - 2 * core, gy)
    east = (lax.rem(gx + 1, 16), gy)
    west = (lax.rem(gx + 15, 16), gy)
    north = (gx, lax.rem(gy + 1, 16))
    south = (gx, lax.rem(gy + 15, 16))
    mine = (y * 2 + core) * 4 + x

    def load(source, target, index):
        copy = pltpu.make_async_copy(source, target, load_sem.at[index])
        copy.start()
        return copy

    load_ids = load(ids_hbm, ids, 0)
    load_rhs = load(rhs_hbm, rhs, 1)
    load_basis = load(basis_hbm, basis, 2)
    load_cinv = load(cinv_hbm, cz.at[z], 3)

    def signal(semaphore, peer):
        pl.semaphore_signal(semaphore, inc=1, device_id=peer, device_id_type=MESH)

    barrier = pltpu.get_barrier_semaphore()
    ring = [ring_peer(d) for d in RING]
    greeted = [plane_peer(o)[1] for o in PLANE] + ring + [east, west, north, south]
    for peer in greeted:
        signal(barrier, peer)

    def send(source, target, send_sem, recv_sem, peer):
        pltpu.make_async_remote_copy(
            src_ref=source, dst_ref=target, send_sem=send_sem, recv_sem=recv_sem,
            device_id=peer, device_id_type=MESH,
        ).start()

    def drain(ref, sem):
        pltpu.make_async_copy(ref, ref, sem).wait()

    def exchange(source, target, send_sem, recv_sem):
        send(source.at[1, 1], target.at[0, 0], send_sem, recv_sem, east)
        send(source.at[0, 0], target.at[1, 1], send_sem, recv_sem, west)
        send(source.at[:, 3], target.at[:, 2], send_sem, recv_sem, north)
        send(source.at[:, 2], target.at[:, 3], send_sem, recv_sem, south)

    def kept(values):
        return [
            (jnp.where(gx > 0, values[0, 0], 0), values[0, 1], jnp.where(gy > 0, values[0, 2], 0),
             jnp.where(gy < 15, values[0, 3], 0)),
            (values[1, 0], jnp.where(gx < 15, values[1, 1], 0), jnp.where(gy > 0, values[1, 2], 0),
             jnp.where(gy < 15, values[1, 3], 0)),
        ]

    load_ids.wait()
    load_rhs.wait()
    load_basis.wait()
    load_inv = load(inv_hbm, inv, 4)
    load_spill = load(spill_hbm, spill, 5)
    load_op = load(op_hbm, op, 6)
    numbers = jnp.concatenate([ids[0], ids[1]], axis=1)
    places = ((numbers & 496) << 1) | ((numbers >> 9) << 4) | (numbers & 15)
    rows = lax.broadcasted_iota(jnp.int32, (NC, 2 * KC), 0)
    scatter = jnp.where(rows == places, 1.0, 0.0).astype(BF16)
    terms = []
    for s in range(2):
        high, rest = split(rhs[s, 0])
        terms.append(dot(basis[s, 0], high) + dot(basis[s, 0], rest))
    high, rest = split(jnp.concatenate(terms, axis=0))
    local_sums = dot(scatter, high) + dot(scatter, rest)
    sbuf[...] = local_sums.astype(BF16).reshape(32, 32, R)

    pl.semaphore_wait(barrier, len(greeted))
    for slot, offset in enumerate(PLANE):
        block, peer = plane_peer(offset)
        send(sbuf.at[block], rbuf.at[slot], rs_send, rs_recv, peer)
    load_cinv.wait()
    for peer in ring:
        send(cz.at[z], cz.at[z], cz_send, cz_recv, peer)
    send(ids.at[1], nids.at[0], i_send, i_recv, east)
    send(ids.at[0], nids.at[1], i_send, i_recv, west)
    send(ids, nids.at[2:4], i_send, i_recv, north)
    send(ids, nids.at[4:6], i_send, i_recv, south)

    load_inv.wait()
    for s in range(2):
        edge = dot(inv[s, 0, OWN:, :], rhs[s, 0].astype(BF16)).astype(BF16).reshape(4, H, R)
        mbuf[s] = edge
        marg[1 - s, s] = edge[1 - s]
    exchange(mbuf, marg, m_send, m_recv)
    heads = [rhs[s, 0].astype(BF16) for s in range(2)]
    for s in range(2):
        corr[s] = dot(inv[s, 0, :OWN, :], heads[s])
    load_spill.wait()
    for s in range(2):
        listed = spill[s, 0]
        listed = jnp.concatenate([listed[d : d + 1] for d in range(4)], axis=1)
        owned = lax.broadcasted_iota(jnp.int32, (OWN, 4 * H), 0)
        spread_mat[s] = jnp.where(owned == listed, 1.0, 0.0).astype(BF16)
        basis_t[s] = jnp.concatenate([basis[s, 0], basis[s, 0]], axis=0).T
    load_op.wait()
    left = lax.broadcasted_iota(jnp.int32, (H, R), 1) < KC
    for s in range(2):
        edge = dot(op[s, 0, OWN:, :], basis_t[s]).reshape(4, H, R)
        for d in range(4):
            half = jnp.where(left if d in (1, 3) else ~left, edge[d], 0.0).astype(BF16)
            mbuf2[s, d, 1] = half
            if d == 1 - s:
                marg2[1 - s, s, 1] = half
        qmat[s, :, 0:R] = dot(op[s, 0, :OWN, :], basis_t[s]).astype(BF16)

    first, second = slice(0, 16), slice(16, 32)

    drain(cz.at[0:7], cz_recv)
    cf[y, core, x] = jnp.concatenate([cz[i].astype(F32) for i in range(ZS)], axis=0).astype(BF16)
    upper, lower = cf.at[y, core, x, first], cf.at[y, core, x, second]
    for d in (2, 1, 3):
        send(upper, upper, c2_send.at[0], c2_recv.at[0], x_peer(d))
        send(lower, lower, c2_send.at[1], c2_recv.at[1], y_peer(d))
    for d in (2, 1, 3):
        send(upper, upper, c3_send.at[0], c3_recv.at[0, d - 1], y_peer(d))
        send(lower, lower, c3_send.at[1], c3_recv.at[1, d - 1], x_peer(d))

    drain(rbuf, rs_recv)
    total = sbuf[mine].astype(F32)
    for slot in range(31):
        total = total + rbuf[slot].astype(F32)
    zs[...] = total.astype(BF16)
    for slot, peer in enumerate(ring):
        send(zs, zr.at[slot], z_send, z_recv, peer)

    drain(mbuf.at[:, 0:3], m_recv)
    received = kept(marg)
    for s in range(2):
        corr[s] = corr[s] + dot(spread_mat[s], jnp.concatenate(received[s], axis=0))
        heads[s] = corr[s].astype(BF16)
        edge = dot(op[s, 0, OWN:, :], heads[s]).astype(BF16).reshape(4, H, R)
        for d in range(4):
            mbuf2[s, d, 0] = edge[d]
        marg2[1 - s, s, 0] = edge[1 - s]
    exchange(mbuf2, marg2, n_send, n_recv)

    drain(cf.at[0, 0, 0:3, first], c2_recv.at[0])
    drain(cf.at[0, 0, 0:3, first], c2_recv.at[1])
    for other in (1, 2, 3):
        xx, yy = lax.rem(x + other, XS), lax.rem(y + other, YS)
        for d in (2, 1, 3):
            upper, lower = cf.at[y, core, xx, first], cf.at[yy, core, x, second]
            send(upper, upper, c3_send.at[0], c3_recv.at[0, d - 1], y_peer(d))
            send(lower, lower, c3_send.at[1], c3_recv.at[1, d - 1], x_peer(d))

    for s in range(2):
        prior[s] = rhs[s, 0] - dot(op[s, 0, :OWN, :], heads[s])
    drain(nids, i_recv)
    lists[0] = jnp.concatenate([ids[0], ids[1]] + [nids[i] for i in range(6)], axis=1)
    send(lists.at[0], lists.at[1], l_send, l_recv, partner)
    rows = lax.broadcasted_iota(jnp.int32, (NC, 8 * KC), 0)
    pick[:, 0 : 8 * KC] = jnp.where(rows == lists[0], 1.0, 0.0).astype(BF16)

    drain(zr, z_recv)
    total = total.astype(BF16).astype(F32)
    for slot in range(7):
        total = total + zr[slot].astype(F32)
    slot_here = y * 4 + x
    low[slot_here] = total.astype(BF16)
    for offset in PLANE:
        if offset[2] == 0:
            send(low.at[slot_here], low.at[slot_here], ag_send, ag_recv, plane_peer(offset)[1])

    drain(lists.at[0], l_recv)
    pick[:, 8 * KC :] = jnp.where(rows == lists[1], 1.0, 0.0).astype(BF16)
    drain(mbuf2.at[:, 0:3], n_recv)
    for s in range(2):
        arrived = [
            jnp.where(gx > 0, marg2[0, 0], 0) if s == 0 else marg2[1, 0],
            marg2[0, 1] if s == 0 else jnp.where(gx < 15, marg2[1, 1], 0),
            jnp.where(gy > 0, marg2[s, 2], 0),
            jnp.where(gy < 15, marg2[s, 3], 0),
        ]
        prior[s] = prior[s] - dot(spread_mat[s], jnp.concatenate([a[0] for a in arrived], axis=0))
        for half in range(2):
            pair = jnp.concatenate([arrived[2 * half][1], arrived[2 * half + 1][1]], axis=0)
            lanes = slice(R * (half + 1), R * (half + 2))
            qmat[s, :, lanes] = dot(spread_mat[s, :, R * half : R * (half + 1)], pair).astype(BF16)

    for d in (1, 3, 2):
        drain(cf.at[0, 0, :, first], c3_recv.at[0, d - 1])
        drain(cf.at[0, 0, :, first], c3_recv.at[1, d - 1])
    for part in (1, 0):
        chosen = dot(cf[:, core].reshape(NC // 2, NC), pick[:, part * 8 * KC : (part + 1) * 8 * KC]).astype(BF16)
        for i in range(4):
            wsel[part, :, i * R : (i + 1) * R] = chosen[i * R : (i + 1) * R].T

    drain(low.at[0:15], ag_recv)
    summed = low[...].reshape(NC // 2, R)
    trade[0] = dot(wsel[1], summed).astype(BF16)
    send(trade.at[0], trade.at[1], c4_send, c4_recv, partner)
    ours = dot(wsel[0], summed)
    drain(trade.at[0], c4_recv)
    picked[...] = ours + trade[1].astype(F32)

    drain(rbuf, rs_send)
    drain(zr, z_send)
    drain(low.at[0:15], ag_send)
    drain(cz.at[0:7], cz_send)
    drain(nids, i_send)
    for i in range(2):
        drain(cf.at[0, 0, 0:3, first], c2_send.at[i])
        drain(cf.at[0:3, 0, :, first], c3_send.at[i])
    drain(lists.at[0], l_send)
    drain(trade.at[0], c4_send)
    drain(mbuf.at[:, 0:3], m_send)
    drain(mbuf2.at[:, 0:3], n_send)


def finish(corr, prior, basis_t, qmat, picked, sol_out, res_out, sol, res, sem):
    parts = [picked[i * KC : (i + 1) * KC].astype(BF16) for i in range(8)]
    beside = ((2, 1, 4, 6), (0, 3, 5, 7))
    copies = []
    for s in range(2):
        high, rest = split(picked[s * KC : (s + 1) * KC])
        both = jnp.concatenate([high, rest], axis=0)
        stack = jnp.concatenate([both] + [parts[i] for i in beside[s]], axis=0)
        res[s] = prior[s] - dot(qmat[s], stack)
        copies.append(pltpu.make_async_copy(res.at[s], res_out.at[s, 0], sem.at[2 * s]))
        copies[-1].start()
        sol[s] = corr[s] + dot(basis_t[s], both)
        copies.append(pltpu.make_async_copy(sol.at[s], sol_out.at[s, 0], sem.at[2 * s + 1]))
        copies[-1].start()
    for copy in copies:
        copy.wait()


def body(adjoint_rhs, local_inverse, local_operator, spill_rows, coarse_basis, coarse_ids, coarse_inverse):
    hbm = pl.BlockSpec(memory_space=pltpu.HBM)
    vmem = pl.BlockSpec(memory_space=pltpu.VMEM)
    dma = pltpu.SemaphoreType.DMA
    out = jax.ShapeDtypeStruct(adjoint_rhs.shape, F32)
    operands = (
        adjoint_rhs, local_inverse, local_operator, spill_rows, coarse_basis, coarse_ids, coarse_inverse
    )
    results = pl.pallas_call(
        kernel,
        out_shape=(
            jax.ShapeDtypeStruct((2, OWN, R), F32),
            jax.ShapeDtypeStruct((2, OWN, R), F32),
            jax.ShapeDtypeStruct((2, OWN, R), BF16),
            jax.ShapeDtypeStruct((2, OWN, 3 * R), BF16),
            jax.ShapeDtypeStruct((8 * KC, R), F32),
        ),
        in_specs=[hbm] * 7,
        out_specs=(vmem,) * 5,
        scratch_shapes=[
            pltpu.VMEM(adjoint_rhs.shape, F32),
            pltpu.VMEM(local_inverse.shape, BF16),
            pltpu.VMEM(local_operator.shape, BF16),
            pltpu.VMEM(spill_rows.shape, jnp.int32),
            pltpu.VMEM(coarse_basis.shape, BF16),
            pltpu.VMEM(coarse_ids.shape, jnp.int32),
            pltpu.VMEM((ZS, 4, NC), BF16),
            pltpu.VMEM((4, 2, 4, 32, NC), BF16),
            pltpu.VMEM((32, 32, R), BF16),
            pltpu.VMEM((31, 32, R), BF16),
            pltpu.VMEM((32, R), BF16),
            pltpu.VMEM((7, 32, R), BF16),
            pltpu.VMEM((16, 32, R), BF16),
            pltpu.VMEM((2, 4, H, R), BF16),
            pltpu.VMEM((2, 4, H, R), BF16),
            pltpu.VMEM((2, 4, 2, H, R), BF16),
            pltpu.VMEM((2, 4, 2, H, R), BF16),
            pltpu.VMEM((6, 1, KC), jnp.int32),
            pltpu.VMEM((2, OWN, 4 * H), BF16),
            pltpu.VMEM((NC, 16 * KC), BF16),
            pltpu.VMEM((2, 8 * KC, NC // 2), BF16),
            pltpu.VMEM((2, 1, 8 * KC), jnp.int32),
            pltpu.VMEM((2, 8 * KC, R), BF16),
            dma((7,)),
            dma(()), dma(()), dma(()), dma(()), dma(()), dma(()),
            dma(()), dma(()), dma((2,)), dma((2,)), dma((2,)), dma((2, 3)), dma(()), dma(()),
            dma(()), dma(()), dma(()), dma(()), dma(()), dma(()), dma(()), dma(()),
        ],
        compiler_params=pltpu.CompilerParams(
            collective_id=0, has_side_effects=True, vmem_limit_bytes=48 * 1024 * 1024
        ),
    )(*[pltpu.with_memory_space_constraint(a, pltpu.HBM) for a in operands])
    return pl.pallas_call(
        finish,
        out_shape=(out, out),
        in_specs=[vmem] * 5,
        out_specs=(hbm, hbm),
        scratch_shapes=[pltpu.VMEM((2, OWN, R), F32), pltpu.VMEM((2, OWN, R), F32), dma((4,))],
        compiler_params=pltpu.CompilerParams(vmem_limit_bytes=16 * 1024 * 1024),
    )(*results)


def solution(mesh):
    in_specs = (
        P("gx", "gy", None, None),
        P("gx", "gy", None, None),
        P("gx", "gy", None, None),
        P("gx", "gy", None, None),
        P("gx", "gy", None, None),
        P("gx", "gy", None),
        P(("gx", "gy"), None),
    )
    out_specs = (P("gx", "gy", None, None), P("gx", "gy", None, None))
    return jax.shard_map(body, mesh=mesh, in_specs=in_specs, out_specs=out_specs, check_vma=False)
```

```python
import functools

import jax
import jax.numpy as jnp
from jax import lax
from jax.experimental import pallas as pl
from jax.experimental.pallas import tpu as pltpu
from jax.sharding import PartitionSpec as P

F32 = jnp.float32
BF16 = jnp.bfloat16
MESH = pl.DeviceIdType.MESH
OWN = 768
H = 64
R = 128
KC = 64
NC = 1024
XS, YS, ZS = 4, 4, 8


def dot(a, b):
    return jnp.dot(a, b, preferred_element_type=F32)


def dot_first(a, b):
    return lax.dot_general(a, b, (((0,), (0,)), ((), ())), preferred_element_type=F32)


def split(value):
    high = value.astype(BF16)
    return high, (value - high.astype(F32)).astype(BF16)


def ring_distance(step, size):
    return min(step, size - step)


PLANE = sorted(
    [(dx, dy, dc) for dx in range(XS) for dy in range(YS) for dc in range(2) if (dx, dy, dc) != (0, 0, 0)],
    key=lambda o: -(ring_distance(o[0], XS) + ring_distance(o[1], YS)),
)
RING = sorted(range(1, ZS), key=lambda dz: -ring_distance(dz, ZS))


def kernel(
    rhs_hbm, inv_hbm, op_hbm, spill_hbm, basis_hbm, ids_hbm, cinv_hbm,
    corr, prior, basis_t, qmat, picked,
    rhs, inv, op, spill, basis, ids, cz, cf,
    sbuf, rbuf, zs, zr, low,
    mbuf, marg, mbuf2, marg2, nids, spread_mat, pick, wsel, lists, trade,
    load_sem, rs_send, rs_recv, z_send, z_recv, ag_send, ag_recv,
    cz_send, cz_recv, c2_send, c2_recv, c3_send, c3_recv, c4_send, c4_recv,
    m_send, m_recv, n_send, n_recv, i_send, i_recv, l_send, l_recv,
):
    gx, gy = lax.axis_index("gx"), lax.axis_index("gy")

    core = lax.rem(gx, 2)
    y = lax.rem(lax.div(gx, 2), YS)
    x = lax.div(gy, 4)
    z = lax.div(gx, 8) * 4 + lax.rem(gy, 4)

    def device(xx, yy, zz, cc):
        return (lax.div(zz, 4) * 8 + yy * 2 + cc, xx * 4 + lax.rem(zz, 4))

    def plane_peer(offset):
        dx, dy, dc = offset
        xx, yy, cc = lax.rem(x + dx, XS), lax.rem(y + dy, YS), lax.rem(core + dc, 2)
        return (yy * 2 + cc) * 4 + xx, device(xx, yy, z, cc)

    def ring_peer(dz):
        return device(x, y, lax.rem(z + dz, ZS), core)

    def x_peer(dx):
        return device(lax.rem(x + dx, XS), y, z, core)

    def y_peer(dy):
        return device(x, lax.rem(y + dy, YS), z, core)

    partner = (gx + 1 - 2 * core, gy)
    east = (lax.rem(gx + 1, 16), gy)
    west = (lax.rem(gx + 15, 16), gy)
    north = (gx, lax.rem(gy + 1, 16))
    south = (gx, lax.rem(gy + 15, 16))
    mine = (y * 2 + core) * 4 + x

    def load(source, target, index):
        copy = pltpu.make_async_copy(source, target, load_sem.at[index])
        copy.start()
        return copy

    load_ids = load(ids_hbm, ids, 0)
    load_rhs = load(rhs_hbm, rhs, 1)
    load_basis = load(basis_hbm, basis, 2)
    load_cinv = load(cinv_hbm, cz.at[z], 3)

    def signal(semaphore, peer):
        pl.semaphore_signal(semaphore, inc=1, device_id=peer, device_id_type=MESH)

    barrier = pltpu.get_barrier_semaphore()
    ring = [ring_peer(d) for d in RING]
    greeted = [plane_peer(o)[1] for o in PLANE] + ring + [east, west, north, south]
    for peer in greeted:
        signal(barrier, peer)

    def send(source, target, send_sem, recv_sem, peer):
        pltpu.make_async_remote_copy(
            src_ref=source, dst_ref=target, send_sem=send_sem, recv_sem=recv_sem,
            device_id=peer, device_id_type=MESH,
        ).start()

    def drain(ref, sem):
        pltpu.make_async_copy(ref, ref, sem).wait()

    def exchange(source, target, send_sem, recv_sem):
        send(source.at[1, 1], target.at[0, 0], send_sem, recv_sem, east)
        send(source.at[0, 0], target.at[1, 1], send_sem, recv_sem, west)
        send(source.at[:, 3], target.at[:, 2], send_sem, recv_sem, north)
        send(source.at[:, 2], target.at[:, 3], send_sem, recv_sem, south)

    def kept(values):
        return [
            (jnp.where(gx > 0, values[0, 0], 0), values[0, 1], jnp.where(gy > 0, values[0, 2], 0),
             jnp.where(gy < 15, values[0, 3], 0)),
            (values[1, 0], jnp.where(gx < 15, values[1, 1], 0), jnp.where(gy > 0, values[1, 2], 0),
             jnp.where(gy < 15, values[1, 3], 0)),
        ]

    load_ids.wait()
    load_rhs.wait()
    load_basis.wait()
    load_inv = load(inv_hbm, inv, 4)
    load_spill = load(spill_hbm, spill, 5)
    load_op = load(op_hbm, op, 6)
    numbers = jnp.concatenate([ids[0], ids[1]], axis=1)
    places = ((numbers & 496) << 1) | ((numbers >> 9) << 4) | (numbers & 15)
    rows = lax.broadcasted_iota(jnp.int32, (NC, 2 * KC), 0)
    scatter = jnp.where(rows == places, 1.0, 0.0).astype(BF16)
    terms = []
    for s in range(2):
        high, rest = split(rhs[s, 0])
        terms.append(dot(basis[s, 0], high) + dot(basis[s, 0], rest))
    high, rest = split(jnp.concatenate(terms, axis=0))
    local_sums = dot(scatter, high) + dot(scatter, rest)
    sbuf[...] = local_sums.astype(BF16).reshape(32, 32, R)

    pl.semaphore_wait(barrier, len(greeted))
    for slot, offset in enumerate(PLANE):
        block, peer = plane_peer(offset)
        send(sbuf.at[block], rbuf.at[slot], rs_send, rs_recv, peer)
    load_cinv.wait()
    for peer in ring:
        send(cz.at[z], cz.at[z], cz_send, cz_recv, peer)
    send(ids.at[1], nids.at[0], i_send, i_recv, east)
    send(ids.at[0], nids.at[1], i_send, i_recv, west)
    send(ids, nids.at[2:4], i_send, i_recv, north)
    send(ids, nids.at[4:6], i_send, i_recv, south)

    load_inv.wait()
    for s in range(2):
        edge = dot(inv[s, 0, OWN:, :], rhs[s, 0].astype(BF16)).astype(BF16).reshape(4, H, R)
        mbuf[s] = edge
        marg[1 - s, s] = edge[1 - s]
    exchange(mbuf, marg, m_send, m_recv)
    heads = [rhs[s, 0].astype(BF16) for s in range(2)]
    for s in range(2):
        corr[s] = dot(inv[s, 0, :OWN, :], heads[s])
    load_spill.wait()
    for s in range(2):
        listed = spill[s, 0]
        listed = jnp.concatenate([listed[d : d + 1] for d in range(4)], axis=1)
        owned = lax.broadcasted_iota(jnp.int32, (OWN, 4 * H), 0)
        spread_mat[s] = jnp.where(owned == listed, 1.0, 0.0).astype(BF16)
        basis_t[s] = jnp.concatenate([basis[s, 0], basis[s, 0]], axis=0).T
    load_op.wait()
    left = lax.broadcasted_iota(jnp.int32, (H, R), 1) < KC
    for s in range(2):
        edge = dot(op[s, 0, OWN:, :], basis_t[s]).reshape(4, H, R)
        for d in range(4):
            half = jnp.where(left if d in (1, 3) else ~left, edge[d], 0.0).astype(BF16)
            mbuf2[s, d, 1] = half
            if d == 1 - s:
                marg2[1 - s, s, 1] = half
        qmat[s, :, 0:R] = dot(op[s, 0, :OWN, :], basis_t[s]).astype(BF16)

    first, second = slice(0, 16), slice(16, 32)

    drain(cz.at[0:7], cz_recv)
    cf[y, core, x] = jnp.concatenate([cz[i].astype(F32) for i in range(ZS)], axis=0).astype(BF16)
    upper, lower = cf.at[y, core, x, first], cf.at[y, core, x, second]
    for d in (2, 1, 3):
        send(upper, upper, c2_send.at[0], c2_recv.at[0], x_peer(d))
        send(lower, lower, c2_send.at[1], c2_recv.at[1], y_peer(d))
    for d in (2, 1, 3):
        send(upper, upper, c3_send.at[0], c3_recv.at[0, d - 1], y_peer(d))
        send(lower, lower, c3_send.at[1], c3_recv.at[1, d - 1], x_peer(d))

    drain(rbuf, rs_recv)
    total = sbuf[mine].astype(F32)
    for slot in range(31):
        total = total + rbuf[slot].astype(F32)
    zs[...] = total.astype(BF16)
    for slot, peer in enumerate(ring):
        send(zs, zr.at[slot], z_send, z_recv, peer)

    drain(mbuf.at[:, 0:3], m_recv)
    received = kept(marg)
    for s in range(2):
        corr[s] = corr[s] + dot(spread_mat[s], jnp.concatenate(received[s], axis=0))
        heads[s] = corr[s].astype(BF16)
        edge = dot(op[s, 0, OWN:, :], heads[s]).astype(BF16).reshape(4, H, R)
        for d in range(4):
            mbuf2[s, d, 0] = edge[d]
        marg2[1 - s, s, 0] = edge[1 - s]
    exchange(mbuf2, marg2, n_send, n_recv)

    drain(cf.at[0, 0, 0:3, first], c2_recv.at[0])
    drain(cf.at[0, 0, 0:3, first], c2_recv.at[1])
    for other in (1, 2, 3):
        xx, yy = lax.rem(x + other, XS), lax.rem(y + other, YS)
        for d in (2, 1, 3):
            upper, lower = cf.at[y, core, xx, first], cf.at[yy, core, x, second]
            send(upper, upper, c3_send.at[0], c3_recv.at[0, d - 1], y_peer(d))
            send(lower, lower, c3_send.at[1], c3_recv.at[1, d - 1], x_peer(d))

    drain(zr, z_recv)
    total = total.astype(BF16).astype(F32)
    for slot in range(7):
        total = total + zr[slot].astype(F32)
    slot_here = y * 4 + x
    low[slot_here] = total.astype(BF16)
    for offset in PLANE:
        if offset[2] == 0:
            send(low.at[slot_here], low.at[slot_here], ag_send, ag_recv, plane_peer(offset)[1])

    drain(nids, i_recv)
    lists[0] = jnp.concatenate([ids[0], ids[1]] + [nids[i] for i in range(6)], axis=1)
    send(lists.at[0], lists.at[1], l_send, l_recv, partner)
    rows = lax.broadcasted_iota(jnp.int32, (NC, 8 * KC), 0)
    pick[:, 0 : 8 * KC] = jnp.where(rows == lists[0], 1.0, 0.0).astype(BF16)
    for s in range(2):
        prior[s] = rhs[s, 0] - dot(op[s, 0, :OWN, :], heads[s])
    drain(lists.at[0], l_recv)
    pick[:, 8 * KC :] = jnp.where(rows == lists[1], 1.0, 0.0).astype(BF16)
    drain(mbuf2.at[:, 0:3], n_recv)
    for s in range(2):
        arrived = [
            jnp.where(gx > 0, marg2[0, 0], 0) if s == 0 else marg2[1, 0],
            marg2[0, 1] if s == 0 else jnp.where(gx < 15, marg2[1, 1], 0),
            jnp.where(gy > 0, marg2[s, 2], 0),
            jnp.where(gy < 15, marg2[s, 3], 0),
        ]
        prior[s] = prior[s] - dot(spread_mat[s], jnp.concatenate([a[0] for a in arrived], axis=0))
        for half in range(2):
            pair = jnp.concatenate([arrived[2 * half][1], arrived[2 * half + 1][1]], axis=0)
            lanes = slice(R * (half + 1), R * (half + 2))
            qmat[s, :, lanes] = dot(spread_mat[s, :, R * half : R * (half + 1)], pair).astype(BF16)

    for d in (1, 3, 2):
        drain(cf.at[0, 0, :, first], c3_recv.at[0, d - 1])
        drain(cf.at[0, 0, :, first], c3_recv.at[1, d - 1])
    for part in (1, 0):
        chosen = dot(cf[:, core].reshape(NC // 2, NC), pick[:, part * 8 * KC : (part + 1) * 8 * KC]).astype(BF16)
        for i in range(4):
            wsel[part, :, i * R : (i + 1) * R] = chosen[i * R : (i + 1) * R].T

    drain(low.at[0:15], ag_recv)
    summed = low[...].reshape(NC // 2, R)
    for part in (slice(0, 4 * KC), slice(4 * KC, 8 * KC)):
        trade[0, part] = dot(wsel[1, part], summed).astype(BF16)
        send(trade.at[0, part], trade.at[1, part], c4_send, c4_recv, partner)
    picked[...] = dot(wsel[0], summed)
    drain(trade.at[0], c4_recv)
    picked[...] += trade[1].astype(F32)

    drain(rbuf, rs_send)
    drain(zr, z_send)
    drain(low.at[0:15], ag_send)
    drain(cz.at[0:7], cz_send)
    drain(nids, i_send)
    for i in range(2):
        drain(cf.at[0, 0, 0:3, first], c2_send.at[i])
        drain(cf.at[0:3, 0, :, first], c3_send.at[i])
    drain(lists.at[0], l_send)
    drain(trade.at[0], c4_send)
    drain(mbuf.at[:, 0:3], m_send)
    drain(mbuf2.at[:, 0:3], n_send)


def finish(corr, prior, basis_t, qmat, picked, sol_out, res_out, sol, res, sem):
    parts = [picked[i * KC : (i + 1) * KC].astype(BF16) for i in range(8)]
    beside = ((2, 1, 4, 6), (0, 3, 5, 7))
    copies = []

    def put(source, target):
        copies.append(pltpu.make_async_copy(source, target, sem.at[len(copies)]))
        copies[-1].start()

    for s in range(2):
        high, rest = split(picked[s * KC : (s + 1) * KC])
        both = jnp.concatenate([high, rest], axis=0)
        stack = jnp.concatenate([both] + [parts[i] for i in beside[s]], axis=0)
        sol[s] = corr[s] + dot(basis_t[s], both)
        put(sol.at[s], sol_out.at[s, 0])
        for part in (slice(0, OWN // 2), slice(OWN // 2, OWN)):
            res[s, part] = prior[s, part] - dot(qmat[s, part], stack)
            put(res.at[s, part], res_out.at[s, 0, part])
    for copy in copies:
        copy.wait()


def body(adjoint_rhs, local_inverse, local_operator, spill_rows, coarse_basis, coarse_ids, coarse_inverse):
    hbm = pl.BlockSpec(memory_space=pltpu.HBM)
    vmem = pl.BlockSpec(memory_space=pltpu.VMEM)
    dma = pltpu.SemaphoreType.DMA
    out = jax.ShapeDtypeStruct(adjoint_rhs.shape, F32)
    operands = (
        adjoint_rhs, local_inverse, local_operator, spill_rows, coarse_basis, coarse_ids, coarse_inverse
    )
    results = pl.pallas_call(
        kernel,
        out_shape=(
            jax.ShapeDtypeStruct((2, OWN, R), F32),
            jax.ShapeDtypeStruct((2, OWN, R), F32),
            jax.ShapeDtypeStruct((2, OWN, R), BF16),
            jax.ShapeDtypeStruct((2, OWN, 3 * R), BF16),
            jax.ShapeDtypeStruct((8 * KC, R), F32),
        ),
        in_specs=[hbm] * 7,
        out_specs=(vmem,) * 5,
        scratch_shapes=[
            pltpu.VMEM(adjoint_rhs.shape, F32),
            pltpu.VMEM(local_inverse.shape, BF16),
            pltpu.VMEM(local_operator.shape, BF16),
            pltpu.VMEM(spill_rows.shape, jnp.int32),
            pltpu.VMEM(coarse_basis.shape, BF16),
            pltpu.VMEM(coarse_ids.shape, jnp.int32),
            pltpu.VMEM((ZS, 4, NC), BF16),
            pltpu.VMEM((4, 2, 4, 32, NC), BF16),
            pltpu.VMEM((32, 32, R), BF16),
            pltpu.VMEM((31, 32, R), BF16),
            pltpu.VMEM((32, R), BF16),
            pltpu.VMEM((7, 32, R), BF16),
            pltpu.VMEM((16, 32, R), BF16),
            pltpu.VMEM((2, 4, H, R), BF16),
            pltpu.VMEM((2, 4, H, R), BF16),
            pltpu.VMEM((2, 4, 2, H, R), BF16),
            pltpu.VMEM((2, 4, 2, H, R), BF16),
            pltpu.VMEM((6, 1, KC), jnp.int32),
            pltpu.VMEM((2, OWN, 4 * H), BF16),
            pltpu.VMEM((NC, 16 * KC), BF16),
            pltpu.VMEM((2, 8 * KC, NC // 2), BF16),
            pltpu.VMEM((2, 1, 8 * KC), jnp.int32),
            pltpu.VMEM((2, 8 * KC, R), BF16),
            dma((7,)),
            dma(()), dma(()), dma(()), dma(()), dma(()), dma(()),
            dma(()), dma(()), dma((2,)), dma((2,)), dma((2,)), dma((2, 3)), dma(()), dma(()),
            dma(()), dma(()), dma(()), dma(()), dma(()), dma(()), dma(()), dma(()),
        ],
        compiler_params=pltpu.CompilerParams(
            collective_id=0, has_side_effects=True, vmem_limit_bytes=48 * 1024 * 1024
        ),
    )(*[pltpu.with_memory_space_constraint(a, pltpu.HBM) for a in operands])
    return pl.pallas_call(
        finish,
        out_shape=(out, out),
        in_specs=[vmem] * 5,
        out_specs=(hbm, hbm),
        scratch_shapes=[pltpu.VMEM((2, OWN, R), F32), pltpu.VMEM((2, OWN, R), F32), dma((6,))],
        compiler_params=pltpu.CompilerParams(vmem_limit_bytes=16 * 1024 * 1024),
    )(*results)


def solution(mesh):
    in_specs = (
        P("gx", "gy", None, None),
        P("gx", "gy", None, None),
        P("gx", "gy", None, None),
        P("gx", "gy", None, None),
        P("gx", "gy", None, None),
        P("gx", "gy", None),
        P(("gx", "gy"), None),
    )
    out_specs = (P("gx", "gy", None, None), P("gx", "gy", None, None))
    return jax.shard_map(body, mesh=mesh, in_specs=in_specs, out_specs=out_specs, check_vma=False)
```

```python
import functools

import jax
import jax.numpy as jnp
from jax import lax
from jax.experimental import pallas as pl
from jax.experimental.pallas import tpu as pltpu
from jax.sharding import PartitionSpec as P

F32 = jnp.float32
BF16 = jnp.bfloat16
MESH = pl.DeviceIdType.MESH
OWN = 768
H = 64
R = 128
KC = 64
NC = 1024
XS, YS, ZS = 4, 4, 8


def dot(a, b):
    return jnp.dot(a, b, preferred_element_type=F32)


def dot_first(a, b):
    return lax.dot_general(a, b, (((0,), (0,)), ((), ())), preferred_element_type=F32)


def split(value):
    high = value.astype(BF16)
    return high, (value - high.astype(F32)).astype(BF16)


def ring_distance(step, size):
    return min(step, size - step)


PLANE = sorted(
    [(dx, dy, dc) for dx in range(XS) for dy in range(YS) for dc in range(2) if (dx, dy, dc) != (0, 0, 0)],
    key=lambda o: -(ring_distance(o[0], XS) + ring_distance(o[1], YS)),
)
RING = sorted(range(1, ZS), key=lambda dz: -ring_distance(dz, ZS))


def kernel(
    rhs_hbm, inv_hbm, op_hbm, spill_hbm, basis_hbm, ids_hbm, cinv_hbm,
    corr, prior, basis_t, qmat, picked,
    rhs, inv, op, spill, basis, ids, cz, cf,
    sbuf, rbuf, zs, zr, low,
    mbuf, marg, mbuf2, marg2, nids, spread_mat, pick, wsel, lists, trade,
    load_sem, rs_send, rs_recv, z_send, z_recv, ag_send, ag_recv,
    cz_send, cz_recv, c2_send, c2_recv, c3_send, c3_recv, c4_send, c4_recv,
    m_send, m_recv, n_send, n_recv, i_send, i_recv, l_send, l_recv,
):
    gx, gy = lax.axis_index("gx"), lax.axis_index("gy")

    core = lax.rem(gx, 2)
    y = lax.rem(lax.div(gx, 2), YS)
    x = lax.div(gy, 4)
    z = lax.div(gx, 8) * 4 + lax.rem(gy, 4)

    def device(xx, yy, zz, cc):
        return (lax.div(zz, 4) * 8 + yy * 2 + cc, xx * 4 + lax.rem(zz, 4))

    def plane_peer(offset):
        dx, dy, dc = offset
        xx, yy, cc = lax.rem(x + dx, XS), lax.rem(y + dy, YS), lax.rem(core + dc, 2)
        return (yy * 2 + cc) * 4 + xx, device(xx, yy, z, cc)

    def ring_peer(dz):
        return device(x, y, lax.rem(z + dz, ZS), core)

    def x_peer(dx):
        return device(lax.rem(x + dx, XS), y, z, core)

    def y_peer(dy):
        return device(x, lax.rem(y + dy, YS), z, core)

    partner = (gx + 1 - 2 * core, gy)
    east = (lax.rem(gx + 1, 16), gy)
    west = (lax.rem(gx + 15, 16), gy)
    north = (gx, lax.rem(gy + 1, 16))
    south = (gx, lax.rem(gy + 15, 16))
    mine = (y * 2 + core) * 4 + x

    def load(source, target, index):
        copy = pltpu.make_async_copy(source, target, load_sem.at[index])
        copy.start()
        return copy

    load_ids = load(ids_hbm, ids, 0)
    load_rhs = load(rhs_hbm, rhs, 1)
    load_basis = load(basis_hbm, basis, 2)
    load_cinv = load(cinv_hbm, cz.at[z], 3)

    def signal(semaphore, peer):
        pl.semaphore_signal(semaphore, inc=1, device_id=peer, device_id_type=MESH)

    barrier = pltpu.get_barrier_semaphore()
    ring = [ring_peer(d) for d in RING]
    greeted = [plane_peer(o)[1] for o in PLANE] + ring + [east, west, north, south]
    for peer in greeted:
        signal(barrier, peer)

    def send(source, target, send_sem, recv_sem, peer):
        pltpu.make_async_remote_copy(
            src_ref=source, dst_ref=target, send_sem=send_sem, recv_sem=recv_sem,
            device_id=peer, device_id_type=MESH,
        ).start()

    def drain(ref, sem):
        pltpu.make_async_copy(ref, ref, sem).wait()

    def exchange(source, target, send_sem, recv_sem):
        send(source.at[1, 1], target.at[0, 0], send_sem, recv_sem, east)
        send(source.at[0, 0], target.at[1, 1], send_sem, recv_sem, west)
        send(source.at[:, 3], target.at[:, 2], send_sem, recv_sem, north)
        send(source.at[:, 2], target.at[:, 3], send_sem, recv_sem, south)

    def kept(values):
        return [
            (jnp.where(gx > 0, values[0, 0], 0), values[0, 1], jnp.where(gy > 0, values[0, 2], 0),
             jnp.where(gy < 15, values[0, 3], 0)),
            (values[1, 0], jnp.where(gx < 15, values[1, 1], 0), jnp.where(gy > 0, values[1, 2], 0),
             jnp.where(gy < 15, values[1, 3], 0)),
        ]

    load_ids.wait()
    load_rhs.wait()
    load_basis.wait()
    load_inv = load(inv_hbm, inv, 4)
    load_spill = load(spill_hbm, spill, 5)
    load_op = load(op_hbm, op, 6)
    numbers = jnp.concatenate([ids[0], ids[1]], axis=1)
    places = ((numbers & 496) << 1) | ((numbers >> 9) << 4) | (numbers & 15)
    rows = lax.broadcasted_iota(jnp.int32, (NC, 2 * KC), 0)
    scatter = jnp.where(rows == places, 1.0, 0.0).astype(BF16)
    terms = []
    for s in range(2):
        high, rest = split(rhs[s, 0])
        terms.append(dot(basis[s, 0], high) + dot(basis[s, 0], rest))
    high, rest = split(jnp.concatenate(terms, axis=0))
    local_sums = dot(scatter, high) + dot(scatter, rest)
    sbuf[...] = local_sums.astype(BF16).reshape(32, 32, R)

    pl.semaphore_wait(barrier, len(greeted))
    for slot, offset in enumerate(PLANE):
        block, peer = plane_peer(offset)
        send(sbuf.at[block], rbuf.at[slot], rs_send, rs_recv, peer)
    load_cinv.wait()
    for peer in ring:
        send(cz.at[z], cz.at[z], cz_send, cz_recv, peer)
    send(ids.at[1], nids.at[0], i_send, i_recv, east)
    send(ids.at[0], nids.at[1], i_send, i_recv, west)
    send(ids, nids.at[2:4], i_send, i_recv, north)
    send(ids, nids.at[4:6], i_send, i_recv, south)

    load_inv.wait()
    for s in range(2):
        edge = dot(inv[s, 0, OWN:, :], rhs[s, 0].astype(BF16)).astype(BF16).reshape(4, H, R)
        mbuf[s] = edge
        marg[1 - s, s] = edge[1 - s]
    exchange(mbuf, marg, m_send, m_recv)
    heads = [rhs[s, 0].astype(BF16) for s in range(2)]
    for s in range(2):
        corr[s] = dot(inv[s, 0, :OWN, :], heads[s])
    load_spill.wait()
    for s in range(2):
        listed = spill[s, 0]
        listed = jnp.concatenate([listed[d : d + 1] for d in range(4)], axis=1)
        owned = lax.broadcasted_iota(jnp.int32, (OWN, 4 * H), 0)
        spread_mat[s] = jnp.where(owned == listed, 1.0, 0.0).astype(BF16)
        basis_t[s] = jnp.concatenate([basis[s, 0], basis[s, 0]], axis=0).T
    load_op.wait()
    left = lax.broadcasted_iota(jnp.int32, (H, R), 1) < KC
    for s in range(2):
        edge = dot(op[s, 0, OWN:, :], basis_t[s]).reshape(4, H, R)
        for d in range(4):
            half = jnp.where(left if d in (1, 3) else ~left, edge[d], 0.0).astype(BF16)
            mbuf2[s, d, 1] = half
            if d == 1 - s:
                marg2[1 - s, s, 1] = half
        qmat[s, :, 0:R] = dot(op[s, 0, :OWN, :], basis_t[s]).astype(BF16)

    first, second = slice(0, 16), slice(16, 32)

    drain(cz.at[0:7], cz_recv)
    cf[y, core, x] = jnp.concatenate([cz[i].astype(F32) for i in range(ZS)], axis=0).astype(BF16)
    upper, lower = cf.at[y, core, x, first], cf.at[y, core, x, second]
    for d in (2, 1, 3):
        send(upper, upper, c2_send.at[0], c2_recv.at[0, d - 1], x_peer(d))
        send(lower, lower, c2_send.at[1], c2_recv.at[1, d - 1], y_peer(d))
    for d in (2, 1, 3):
        send(upper, upper, c3_send.at[0], c3_recv.at[0, d - 1], y_peer(d))
        send(lower, lower, c3_send.at[1], c3_recv.at[1, d - 1], x_peer(d))

    drain(rbuf, rs_recv)
    total = sbuf[mine].astype(F32)
    for slot in range(31):
        total = total + rbuf[slot].astype(F32)
    zs[...] = total.astype(BF16)
    for slot, peer in enumerate(ring):
        send(zs, zr.at[slot], z_send, z_recv, peer)

    drain(mbuf.at[:, 0:3], m_recv)
    received = kept(marg)
    for s in range(2):
        corr[s] = corr[s] + dot(spread_mat[s], jnp.concatenate(received[s], axis=0))
        heads[s] = corr[s].astype(BF16)
        edge = dot(op[s, 0, OWN:, :], heads[s]).astype(BF16).reshape(4, H, R)
        for d in range(4):
            mbuf2[s, d, 0] = edge[d]
        marg2[1 - s, s, 0] = edge[1 - s]
    exchange(mbuf2, marg2, n_send, n_recv)

    for back in (1, 3, 2):
        drain(cf.at[0, 0, 0, first], c2_recv.at[0, back - 1])
        drain(cf.at[0, 0, 0, first], c2_recv.at[1, back - 1])
        xx, yy = lax.rem(x + XS - back, XS), lax.rem(y + YS - back, YS)
        for d in (2, 1, 3):
            upper, lower = cf.at[y, core, xx, first], cf.at[yy, core, x, second]
            send(upper, upper, c3_send.at[0], c3_recv.at[0, d - 1], y_peer(d))
            send(lower, lower, c3_send.at[1], c3_recv.at[1, d - 1], x_peer(d))

    drain(zr, z_recv)
    total = total.astype(BF16).astype(F32)
    for slot in range(7):
        total = total + zr[slot].astype(F32)
    slot_here = y * 4 + x
    low[slot_here] = total.astype(BF16)
    for offset in PLANE:
        if offset[2] == 0:
            send(low.at[slot_here], low.at[slot_here], ag_send, ag_recv, plane_peer(offset)[1])

    drain(nids, i_recv)
    lists[0] = jnp.concatenate([ids[0], ids[1]] + [nids[i] for i in range(6)], axis=1)
    send(lists.at[0], lists.at[1], l_send, l_recv, partner)
    rows = lax.broadcasted_iota(jnp.int32, (NC, 8 * KC), 0)
    pick[:, 0 : 8 * KC] = jnp.where(rows == lists[0], 1.0, 0.0).astype(BF16)
    for s in range(2):
        prior[s] = rhs[s, 0] - dot(op[s, 0, :OWN, :], heads[s])
    drain(lists.at[0], l_recv)
    pick[:, 8 * KC :] = jnp.where(rows == lists[1], 1.0, 0.0).astype(BF16)
    drain(mbuf2.at[:, 0:3], n_recv)
    for s in range(2):
        arrived = [
            jnp.where(gx > 0, marg2[0, 0], 0) if s == 0 else marg2[1, 0],
            marg2[0, 1] if s == 0 else jnp.where(gx < 15, marg2[1, 1], 0),
            jnp.where(gy > 0, marg2[s, 2], 0),
            jnp.where(gy < 15, marg2[s, 3], 0),
        ]
        prior[s] = prior[s] - dot(spread_mat[s], jnp.concatenate([a[0] for a in arrived], axis=0))
        for half in range(2):
            pair = jnp.concatenate([arrived[2 * half][1], arrived[2 * half + 1][1]], axis=0)
            lanes = slice(R * (half + 1), R * (half + 2))
            qmat[s, :, lanes] = dot(spread_mat[s, :, R * half : R * (half + 1)], pair).astype(BF16)

    for d in (1, 3, 2):
        drain(cf.at[0, 0, :, first], c3_recv.at[0, d - 1])
        drain(cf.at[0, 0, :, first], c3_recv.at[1, d - 1])
    for part in (1, 0):
        chosen = dot(cf[:, core].reshape(NC // 2, NC), pick[:, part * 8 * KC : (part + 1) * 8 * KC]).astype(BF16)
        for i in range(4):
            wsel[part, :, i * R : (i + 1) * R] = chosen[i * R : (i + 1) * R].T

    drain(low.at[0:15], ag_recv)
    summed = low[...].reshape(NC // 2, R)
    for part in (slice(0, 4 * KC), slice(4 * KC, 8 * KC)):
        trade[0, part] = dot(wsel[1, part], summed).astype(BF16)
        send(trade.at[0, part], trade.at[1, part], c4_send, c4_recv, partner)
    picked[...] = dot(wsel[0], summed)
    drain(trade.at[0], c4_recv)
    picked[...] += trade[1].astype(F32)

    drain(rbuf, rs_send)
    drain(zr, z_send)
    drain(low.at[0:15], ag_send)
    drain(cz.at[0:7], cz_send)
    drain(nids, i_send)
    for i in range(2):
        drain(cf.at[0, 0, 0:3, first], c2_send.at[i])
        drain(cf.at[0:3, 0, :, first], c3_send.at[i])
    drain(lists.at[0], l_send)
    drain(trade.at[0], c4_send)
    drain(mbuf.at[:, 0:3], m_send)
    drain(mbuf2.at[:, 0:3], n_send)


def finish(corr, prior, basis_t, qmat, picked, sol_out, res_out, sol, res, sem):
    parts = [picked[i * KC : (i + 1) * KC].astype(BF16) for i in range(8)]
    beside = ((2, 1, 4, 6), (0, 3, 5, 7))
    copies = []

    def put(source, target):
        copies.append(pltpu.make_async_copy(source, target, sem.at[len(copies)]))
        copies[-1].start()

    for s in range(2):
        high, rest = split(picked[s * KC : (s + 1) * KC])
        both = jnp.concatenate([high, rest], axis=0)
        stack = jnp.concatenate([both] + [parts[i] for i in beside[s]], axis=0)
        sol[s] = corr[s] + dot(basis_t[s], both)
        put(sol.at[s], sol_out.at[s, 0])
        for part in (slice(0, OWN // 2), slice(OWN // 2, OWN)):
            res[s, part] = prior[s, part] - dot(qmat[s, part], stack)
            put(res.at[s, part], res_out.at[s, 0, part])
    for copy in copies:
        copy.wait()


def body(adjoint_rhs, local_inverse, local_operator, spill_rows, coarse_basis, coarse_ids, coarse_inverse):
    hbm = pl.BlockSpec(memory_space=pltpu.HBM)
    vmem = pl.BlockSpec(memory_space=pltpu.VMEM)
    dma = pltpu.SemaphoreType.DMA
    out = jax.ShapeDtypeStruct(adjoint_rhs.shape, F32)
    operands = (
        adjoint_rhs, local_inverse, local_operator, spill_rows, coarse_basis, coarse_ids, coarse_inverse
    )
    results = pl.pallas_call(
        kernel,
        out_shape=(
            jax.ShapeDtypeStruct((2, OWN, R), F32),
            jax.ShapeDtypeStruct((2, OWN, R), F32),
            jax.ShapeDtypeStruct((2, OWN, R), BF16),
            jax.ShapeDtypeStruct((2, OWN, 3 * R), BF16),
            jax.ShapeDtypeStruct((8 * KC, R), F32),
        ),
        in_specs=[hbm] * 7,
        out_specs=(vmem,) * 5,
        scratch_shapes=[
            pltpu.VMEM(adjoint_rhs.shape, F32),
            pltpu.VMEM(local_inverse.shape, BF16),
            pltpu.VMEM(local_operator.shape, BF16),
            pltpu.VMEM(spill_rows.shape, jnp.int32),
            pltpu.VMEM(coarse_basis.shape, BF16),
            pltpu.VMEM(coarse_ids.shape, jnp.int32),
            pltpu.VMEM((ZS, 4, NC), BF16),
            pltpu.VMEM((4, 2, 4, 32, NC), BF16),
            pltpu.VMEM((32, 32, R), BF16),
            pltpu.VMEM((31, 32, R), BF16),
            pltpu.VMEM((32, R), BF16),
            pltpu.VMEM((7, 32, R), BF16),
            pltpu.VMEM((16, 32, R), BF16),
            pltpu.VMEM((2, 4, H, R), BF16),
            pltpu.VMEM((2, 4, H, R), BF16),
            pltpu.VMEM((2, 4, 2, H, R), BF16),
            pltpu.VMEM((2, 4, 2, H, R), BF16),
            pltpu.VMEM((6, 1, KC), jnp.int32),
            pltpu.VMEM((2, OWN, 4 * H), BF16),
            pltpu.VMEM((NC, 16 * KC), BF16),
            pltpu.VMEM((2, 8 * KC, NC // 2), BF16),
            pltpu.VMEM((2, 1, 8 * KC), jnp.int32),
            pltpu.VMEM((2, 8 * KC, R), BF16),
            dma((7,)),
            dma(()), dma(()), dma(()), dma(()), dma(()), dma(()),
            dma(()), dma(()), dma((2,)), dma((2, 3)), dma((2,)), dma((2, 3)), dma(()), dma(()),
            dma(()), dma(()), dma(()), dma(()), dma(()), dma(()), dma(()), dma(()),
        ],
        compiler_params=pltpu.CompilerParams(
            collective_id=0, has_side_effects=True, vmem_limit_bytes=48 * 1024 * 1024
        ),
    )(*[pltpu.with_memory_space_constraint(a, pltpu.HBM) for a in operands])
    return pl.pallas_call(
        finish,
        out_shape=(out, out),
        in_specs=[vmem] * 5,
        out_specs=(hbm, hbm),
        scratch_shapes=[pltpu.VMEM((2, OWN, R), F32), pltpu.VMEM((2, OWN, R), F32), dma((6,))],
        compiler_params=pltpu.CompilerParams(vmem_limit_bytes=16 * 1024 * 1024),
    )(*results)


def solution(mesh):
    in_specs = (
        P("gx", "gy", None, None),
        P("gx", "gy", None, None),
        P("gx", "gy", None, None),
        P("gx", "gy", None, None),
        P("gx", "gy", None, None),
        P("gx", "gy", None),
        P(("gx", "gy"), None),
    )
    out_specs = (P("gx", "gy", None, None), P("gx", "gy", None, None))
    return jax.shard_map(body, mesh=mesh, in_specs=in_specs, out_specs=out_specs, check_vma=False)
```

```python
import functools

import jax
import jax.numpy as jnp
from jax import lax
from jax.experimental import pallas as pl
from jax.experimental.pallas import tpu as pltpu
from jax.sharding import PartitionSpec as P

F32 = jnp.float32
BF16 = jnp.bfloat16
MESH = pl.DeviceIdType.MESH
OWN = 768
H = 64
R = 128
KC = 64
NC = 1024
XS, YS, ZS = 4, 4, 8


def dot(a, b):
    return jnp.dot(a, b, preferred_element_type=F32)


def dot_first(a, b):
    return lax.dot_general(a, b, (((0,), (0,)), ((), ())), preferred_element_type=F32)


def split(value):
    high = value.astype(BF16)
    return high, (value - high.astype(F32)).astype(BF16)


def ring_distance(step, size):
    return min(step, size - step)


PLANE = sorted(
    [(dx, dy, dc) for dx in range(XS) for dy in range(YS) for dc in range(2) if (dx, dy, dc) != (0, 0, 0)],
    key=lambda o: -(ring_distance(o[0], XS) + ring_distance(o[1], YS)),
)
RING = sorted(range(1, ZS), key=lambda dz: -ring_distance(dz, ZS))


def kernel(
    rhs_hbm, inv_hbm, op_hbm, spill_hbm, basis_hbm, ids_hbm, cinv_hbm,
    corr, prior, basis_t, qmat, picked,
    rhs, inv, op, spill, basis, ids, cz, cf,
    sbuf, rbuf, zs, zr, low,
    mbuf, marg, mbuf2, marg2, nids, spread_mat, pick, wsel, lists, trade,
    load_sem, rs_send, rs_recv, z_send, z_recv, ag_send, ag_recv,
    cz_send, cz_recv, c2_send, c2_recv, c3_send, c3_recv, c4_send, c4_recv,
    m_send, m_recv, n_send, n_recv, i_send, i_recv, l_send, l_recv,
):
    gx, gy = lax.axis_index("gx"), lax.axis_index("gy")

    core = lax.rem(gx, 2)
    y = lax.rem(lax.div(gx, 2), YS)
    x = lax.div(gy, 4)
    z = lax.div(gx, 8) * 4 + lax.rem(gy, 4)

    def device(xx, yy, zz, cc):
        return (lax.div(zz, 4) * 8 + yy * 2 + cc, xx * 4 + lax.rem(zz, 4))

    def plane_peer(offset):
        dx, dy, dc = offset
        xx, yy, cc = lax.rem(x + dx, XS), lax.rem(y + dy, YS), lax.rem(core + dc, 2)
        return (yy * 2 + cc) * 4 + xx, device(xx, yy, z, cc)

    def ring_peer(dz):
        return device(x, y, lax.rem(z + dz, ZS), core)

    def x_peer(dx):
        return device(lax.rem(x + dx, XS), y, z, core)

    def y_peer(dy):
        return device(x, lax.rem(y + dy, YS), z, core)

    partner = (gx + 1 - 2 * core, gy)
    east = (lax.rem(gx + 1, 16), gy)
    west = (lax.rem(gx + 15, 16), gy)
    north = (gx, lax.rem(gy + 1, 16))
    south = (gx, lax.rem(gy + 15, 16))
    mine = (y * 2 + core) * 4 + x

    def load(source, target, index):
        copy = pltpu.make_async_copy(source, target, load_sem.at[index])
        copy.start()
        return copy

    load_ids = load(ids_hbm, ids, 0)
    load_rhs = load(rhs_hbm, rhs, 1)
    load_basis = load(basis_hbm, basis, 2)
    load_cinv = load(cinv_hbm, cz.at[z], 3)

    def signal(semaphore, peer):
        pl.semaphore_signal(semaphore, inc=1, device_id=peer, device_id_type=MESH)

    barrier = pltpu.get_barrier_semaphore()
    ring = [ring_peer(d) for d in RING]
    greeted = [plane_peer(o)[1] for o in PLANE] + ring + [east, west, north, south]
    for peer in greeted:
        signal(barrier, peer)

    def send(source, target, send_sem, recv_sem, peer):
        pltpu.make_async_remote_copy(
            src_ref=source, dst_ref=target, send_sem=send_sem, recv_sem=recv_sem,
            device_id=peer, device_id_type=MESH,
        ).start()

    def drain(ref, sem):
        pltpu.make_async_copy(ref, ref, sem).wait()

    def exchange(source, target, send_sem, recv_sem):
        send(source.at[1, 1], target.at[0, 0], send_sem, recv_sem, east)
        send(source.at[0, 0], target.at[1, 1], send_sem, recv_sem, west)
        send(source.at[:, 3], target.at[:, 2], send_sem, recv_sem, north)
        send(source.at[:, 2], target.at[:, 3], send_sem, recv_sem, south)

    def kept(values):
        return [
            (jnp.where(gx > 0, values[0, 0], 0), values[0, 1], jnp.where(gy > 0, values[0, 2], 0),
             jnp.where(gy < 15, values[0, 3], 0)),
            (values[1, 0], jnp.where(gx < 15, values[1, 1], 0), jnp.where(gy > 0, values[1, 2], 0),
             jnp.where(gy < 15, values[1, 3], 0)),
        ]

    load_ids.wait()
    load_rhs.wait()
    load_basis.wait()
    load_inv = load(inv_hbm, inv, 4)
    load_spill = load(spill_hbm, spill, 5)
    load_op = load(op_hbm, op, 6)
    numbers = jnp.concatenate([ids[0], ids[1]], axis=1)
    places = ((numbers & 496) << 1) | ((numbers >> 9) << 4) | (numbers & 15)
    rows = lax.broadcasted_iota(jnp.int32, (NC, 2 * KC), 0)
    scatter = jnp.where(rows == places, 1.0, 0.0).astype(BF16)
    terms = []
    for s in range(2):
        high, rest = split(rhs[s, 0])
        terms.append(dot(basis[s, 0], high) + dot(basis[s, 0], rest))
    high, rest = split(jnp.concatenate(terms, axis=0))
    local_sums = dot(scatter, high) + dot(scatter, rest)
    sbuf[...] = local_sums.astype(BF16).reshape(32, 32, R)

    pl.semaphore_wait(barrier, len(greeted))
    for slot, offset in enumerate(PLANE):
        block, peer = plane_peer(offset)
        send(sbuf.at[block], rbuf.at[slot], rs_send, rs_recv, peer)
    load_cinv.wait()
    for peer in ring:
        send(cz.at[z], cz.at[z], cz_send, cz_recv, peer)
    send(ids.at[1], nids.at[0], i_send, i_recv, east)
    send(ids.at[0], nids.at[1], i_send, i_recv, west)
    send(ids, nids.at[2:4], i_send, i_recv, north)
    send(ids, nids.at[4:6], i_send, i_recv, south)

    load_inv.wait()
    for s in range(2):
        edge = dot(inv[s, 0, OWN:, :], rhs[s, 0].astype(BF16)).astype(BF16).reshape(4, H, R)
        mbuf[s] = edge
        marg[1 - s, s] = edge[1 - s]
    exchange(mbuf, marg, m_send, m_recv)
    heads = [rhs[s, 0].astype(BF16) for s in range(2)]
    for s in range(2):
        corr[s] = dot(inv[s, 0, :OWN, :], heads[s])
    load_spill.wait()
    for s in range(2):
        listed = spill[s, 0]
        listed = jnp.concatenate([listed[d : d + 1] for d in range(4)], axis=1)
        owned = lax.broadcasted_iota(jnp.int32, (OWN, 4 * H), 0)
        spread_mat[s] = jnp.where(owned == listed, 1.0, 0.0).astype(BF16)
        basis_t[s] = jnp.concatenate([basis[s, 0], basis[s, 0]], axis=0).T
    load_op.wait()
    left = lax.broadcasted_iota(jnp.int32, (H, R), 1) < KC
    for s in range(2):
        edge = dot(op[s, 0, OWN:, :], basis_t[s]).reshape(4, H, R)
        for d in range(4):
            half = jnp.where(left if d in (1, 3) else ~left, edge[d], 0.0).astype(BF16)
            mbuf2[s, d, 1] = half
            if d == 1 - s:
                marg2[1 - s, s, 1] = half
        qmat[s, :, 0:R] = dot(op[s, 0, :OWN, :], basis_t[s]).astype(BF16)

    first, second = slice(0, 16), slice(16, 32)

    drain(cz.at[0:7], cz_recv)
    cf[y, core, x] = jnp.concatenate([cz[i].astype(F32) for i in range(ZS)], axis=0).astype(BF16)
    upper, lower = cf.at[y, core, x, first], cf.at[y, core, x, second]
    for d in (2, 1, 3):
        send(upper, upper, c2_send.at[0], c2_recv.at[0, d - 1], x_peer(d))
        send(lower, lower, c2_send.at[1], c2_recv.at[1, d - 1], y_peer(d))
    for d in (2, 1, 3):
        send(upper, upper, c3_send.at[0], c3_recv.at[0, d - 1], y_peer(d))
        send(lower, lower, c3_send.at[1], c3_recv.at[1, d - 1], x_peer(d))

    drain(rbuf, rs_recv)
    total = sbuf[mine].astype(F32)
    for slot in range(31):
        total = total + rbuf[slot].astype(F32)
    zs[...] = total.astype(BF16)
    for slot, peer in enumerate(ring):
        send(zs, zr.at[slot], z_send, z_recv, peer)

    drain(mbuf.at[:, 0:3], m_recv)
    received = kept(marg)
    for s in range(2):
        corr[s] = corr[s] + dot(spread_mat[s], jnp.concatenate(received[s], axis=0))
        heads[s] = corr[s].astype(BF16)
        edge = dot(op[s, 0, OWN:, :], heads[s]).astype(BF16).reshape(4, H, R)
        for d in range(4):
            mbuf2[s, d, 0] = edge[d]
        marg2[1 - s, s, 0] = edge[1 - s]
    exchange(mbuf2, marg2, n_send, n_recv)

    for back in (1, 3, 2):
        drain(cf.at[0, 0, 0, first], c2_recv.at[0, back - 1])
        drain(cf.at[0, 0, 0, first], c2_recv.at[1, back - 1])
        xx, yy = lax.rem(x + XS - back, XS), lax.rem(y + YS - back, YS)
        for d in (2, 1, 3):
            upper, lower = cf.at[y, core, xx, first], cf.at[yy, core, x, second]
            send(upper, upper, c3_send.at[0], c3_recv.at[0, d - 1], y_peer(d))
            send(lower, lower, c3_send.at[1], c3_recv.at[1, d - 1], x_peer(d))

    drain(zr, z_recv)
    total = total.astype(BF16).astype(F32)
    for slot in range(7):
        total = total + zr[slot].astype(F32)
    slot_here = y * 4 + x
    low[slot_here] = total.astype(BF16)
    for offset in PLANE:
        if offset[2] == 0:
            send(low.at[slot_here], low.at[slot_here], ag_send, ag_recv, plane_peer(offset)[1])

    drain(nids, i_recv)
    lists[0] = jnp.concatenate([ids[0], ids[1]] + [nids[i] for i in range(6)], axis=1)
    send(lists.at[0], lists.at[1], l_send, l_recv, partner)
    rows = lax.broadcasted_iota(jnp.int32, (NC, 8 * KC), 0)
    pick[:, 0 : 8 * KC] = jnp.where(rows == lists[0], 1.0, 0.0).astype(BF16)
    for s in range(2):
        prior[s] = rhs[s, 0] - dot(op[s, 0, :OWN, :], heads[s])
    drain(lists.at[0], l_recv)
    pick[:, 8 * KC :] = jnp.where(rows == lists[1], 1.0, 0.0).astype(BF16)
    drain(mbuf2.at[:, 0:3], n_recv)
    for s in range(2):
        arrived = [
            jnp.where(gx > 0, marg2[0, 0], 0) if s == 0 else marg2[1, 0],
            marg2[0, 1] if s == 0 else jnp.where(gx < 15, marg2[1, 1], 0),
            jnp.where(gy > 0, marg2[s, 2], 0),
            jnp.where(gy < 15, marg2[s, 3], 0),
        ]
        prior[s] = prior[s] - dot(spread_mat[s], jnp.concatenate([a[0] for a in arrived], axis=0))
        for half in range(2):
            pair = jnp.concatenate([arrived[2 * half][1], arrived[2 * half + 1][1]], axis=0)
            lanes = slice(R * (half + 1), R * (half + 2))
            qmat[s, :, lanes] = dot(spread_mat[s, :, R * half : R * (half + 1)], pair).astype(BF16)

    for d in (1, 3, 2):
        drain(cf.at[0, 0, :, first], c3_recv.at[0, d - 1])
        drain(cf.at[0, 0, :, first], c3_recv.at[1, d - 1])
    for part in (1, 0):
        chosen = dot(cf[:, core].reshape(NC // 2, NC), pick[:, part * 8 * KC : (part + 1) * 8 * KC]).astype(BF16)
        for i in range(4):
            wsel[part, :, i * R : (i + 1) * R] = chosen[i * R : (i + 1) * R].T

    drain(low.at[0:15], ag_recv)
    summed = low[...].reshape(NC // 2, R)
    for part in (slice(0, 4 * KC), slice(4 * KC, 6 * KC), slice(6 * KC, 8 * KC)):
        trade[0, part] = dot(wsel[1, part], summed).astype(BF16)
        send(trade.at[0, part], trade.at[1, part], c4_send, c4_recv, partner)
    picked[...] = dot(wsel[0], summed)
    drain(trade.at[0], c4_recv)
    picked[...] += trade[1].astype(F32)

    drain(rbuf, rs_send)
    drain(zr, z_send)
    drain(low.at[0:15], ag_send)
    drain(cz.at[0:7], cz_send)
    drain(nids, i_send)
    for i in range(2):
        drain(cf.at[0, 0, 0:3, first], c2_send.at[i])
        drain(cf.at[0:3, 0, :, first], c3_send.at[i])
    drain(lists.at[0], l_send)
    drain(trade.at[0], c4_send)
    drain(mbuf.at[:, 0:3], m_send)
    drain(mbuf2.at[:, 0:3], n_send)


def finish(corr, prior, basis_t, qmat, picked, sol_out, res_out, sol, res, sem):
    parts = [picked[i * KC : (i + 1) * KC].astype(BF16) for i in range(8)]
    beside = ((2, 1, 4, 6), (0, 3, 5, 7))
    copies = []

    def put(source, target):
        copies.append(pltpu.make_async_copy(source, target, sem.at[len(copies)]))
        copies[-1].start()

    for s in range(2):
        high, rest = split(picked[s * KC : (s + 1) * KC])
        both = jnp.concatenate([high, rest], axis=0)
        stack = jnp.concatenate([both] + [parts[i] for i in beside[s]], axis=0)
        sol[s] = corr[s] + dot(basis_t[s], both)
        put(sol.at[s], sol_out.at[s, 0])
        for part in (slice(0, OWN // 2), slice(OWN // 2, OWN)):
            res[s, part] = prior[s, part] - dot(qmat[s, part], stack)
            put(res.at[s, part], res_out.at[s, 0, part])
    for copy in copies:
        copy.wait()


def body(adjoint_rhs, local_inverse, local_operator, spill_rows, coarse_basis, coarse_ids, coarse_inverse):
    hbm = pl.BlockSpec(memory_space=pltpu.HBM)
    vmem = pl.BlockSpec(memory_space=pltpu.VMEM)
    dma = pltpu.SemaphoreType.DMA
    out = jax.ShapeDtypeStruct(adjoint_rhs.shape, F32)
    operands = (
        adjoint_rhs, local_inverse, local_operator, spill_rows, coarse_basis, coarse_ids, coarse_inverse
    )
    results = pl.pallas_call(
        kernel,
        out_shape=(
            jax.ShapeDtypeStruct((2, OWN, R), F32),
            jax.ShapeDtypeStruct((2, OWN, R), F32),
            jax.ShapeDtypeStruct((2, OWN, R), BF16),
            jax.ShapeDtypeStruct((2, OWN, 3 * R), BF16),
            jax.ShapeDtypeStruct((8 * KC, R), F32),
        ),
        in_specs=[hbm] * 7,
        out_specs=(vmem,) * 5,
        scratch_shapes=[
            pltpu.VMEM(adjoint_rhs.shape, F32),
            pltpu.VMEM(local_inverse.shape, BF16),
            pltpu.VMEM(local_operator.shape, BF16),
            pltpu.VMEM(spill_rows.shape, jnp.int32),
            pltpu.VMEM(coarse_basis.shape, BF16),
            pltpu.VMEM(coarse_ids.shape, jnp.int32),
            pltpu.VMEM((ZS, 4, NC), BF16),
            pltpu.VMEM((4, 2, 4, 32, NC), BF16),
            pltpu.VMEM((32, 32, R), BF16),
            pltpu.VMEM((31, 32, R), BF16),
            pltpu.VMEM((32, R), BF16),
            pltpu.VMEM((7, 32, R), BF16),
            pltpu.VMEM((16, 32, R), BF16),
            pltpu.VMEM((2, 4, H, R), BF16),
            pltpu.VMEM((2, 4, H, R), BF16),
            pltpu.VMEM((2, 4, 2, H, R), BF16),
            pltpu.VMEM((2, 4, 2, H, R), BF16),
            pltpu.VMEM((6, 1, KC), jnp.int32),
            pltpu.VMEM((2, OWN, 4 * H), BF16),
            pltpu.VMEM((NC, 16 * KC), BF16),
            pltpu.VMEM((2, 8 * KC, NC // 2), BF16),
            pltpu.VMEM((2, 1, 8 * KC), jnp.int32),
            pltpu.VMEM((2, 8 * KC, R), BF16),
            dma((7,)),
            dma(()), dma(()), dma(()), dma(()), dma(()), dma(()),
            dma(()), dma(()), dma((2,)), dma((2, 3)), dma((2,)), dma((2, 3)), dma(()), dma(()),
            dma(()), dma(()), dma(()), dma(()), dma(()), dma(()), dma(()), dma(()),
        ],
        compiler_params=pltpu.CompilerParams(
            collective_id=0, has_side_effects=True, vmem_limit_bytes=48 * 1024 * 1024
        ),
    )(*[pltpu.with_memory_space_constraint(a, pltpu.HBM) for a in operands])
    return pl.pallas_call(
        finish,
        out_shape=(out, out),
        in_specs=[vmem] * 5,
        out_specs=(hbm, hbm),
        scratch_shapes=[pltpu.VMEM((2, OWN, R), F32), pltpu.VMEM((2, OWN, R), F32), dma((6,))],
        compiler_params=pltpu.CompilerParams(vmem_limit_bytes=16 * 1024 * 1024),
    )(*results)


def solution(mesh):
    in_specs = (
        P("gx", "gy", None, None),
        P("gx", "gy", None, None),
        P("gx", "gy", None, None),
        P("gx", "gy", None, None),
        P("gx", "gy", None, None),
        P("gx", "gy", None),
        P(("gx", "gy"), None),
    )
    out_specs = (P("gx", "gy", None, None), P("gx", "gy", None, None))
    return jax.shard_map(body, mesh=mesh, in_specs=in_specs, out_specs=out_specs, check_vma=False)
```
